32 devices in a mesh: dp: 16 (over z, x, core), section: 2 (over y).
Axes of the slice: x: 2, y: 2, z: 4, core: 2. Of those that a mesh axis runs over, the one named last changes fastest.
Arguments:
- section_inputs: bfloat16 [2, 128, 8, 4, 4, 768], P('section', 'dp'), may hold values from -6 to 6
- cotangent: bfloat16 [128, 8, 4, 4, 128], P('dp'), may hold values from -6 to 6
- sessions: int32 [128], P('dp'), may hold values from 0 to 3
- point_weight: bfloat16 [2, 768, 768], P('section', 'dp'), may hold values from -0.21875 to 0.21875
- spatial_kernel: float32 [2, 9, 768], P('section'), may hold values from -1.5 to 1.5
- temporal_kernel: float32 [2, 5, 768], P('section'), may hold values from -2 to 2
- readout: bfloat16 [4, 128, 768], replicated, may hold values from -0.5 to 0.5
Outputs:
- point_grads: float32 [2, 768, 768], P('section', 'dp')
- spatial_grads: float32 [2, 9, 768], P('section')
- temporal_grads: float32 [2, 5, 768], P('section')
The draws below stay inside these ranges and needn't reach their ends.
All inputs are finite; a program needn't handle non-finite values.
Results may differ from the reference program's by a relative error of at most 0.0071.
Values may be sent and summed in bfloat16 or wider, within the bound.
A program may use at most 64 MiB of HBM per device.

```python
import math
import jax
import jax.numpy as jnp
from jax import lax

CH = 768
REGIONS = 128
SESSIONS = 4
TAPS = 5
SIDE = 4
FRAMES = 8
CLIPS = 128
SECTIONS = 2


def set_ends(result, own_key, low, largest):
    longest = result.shape.index(max(result.shape))
    spots = []
    for shift in (0, 1):
        where = [jax.random.randint(jax.random.fold_in(own_key, axis), (), 0, length) for axis, length in enumerate(result.shape)]
        where[longest] = (where[longest] + shift) % result.shape[longest]
        spots.append(tuple(where))
    return result.at[spots[0]].set(low).at[spots[1]].set(largest)


def shard_levels(own_key, extent, shards, low, top_value):
    def one(dim, shards_of):
        heights = jax.random.uniform(jax.random.fold_in(jax.random.fold_in(own_key, 6), dim), (shards_of,), jnp.float32, low / len(shards), top_value / len(shards))
        return jnp.repeat(jnp.exp(heights), extent[dim] // shards_of).reshape((-1,) + (1,) * (len(extent) - dim - 1))

    factor_of = one(*shards[0])
    for cut in shards[1:]:
        factor_of = factor_of * one(*cut)
    return factor_of


def normal_values(key, shape, scale, most, split=(), dtype=jnp.bfloat16):
    values = scale * jax.random.normal(key, shape, jnp.float32)
    if split:
        values = values * shard_levels(key, shape, split, -0.22, 0.18)
    return jnp.clip(values, -most, most).astype(dtype)


def setup_inputs(seed: int = 0) -> dict:
    keys = jax.random.split(jax.random.key(seed), 8)
    return {
        "section_inputs": normal_values(keys[0], (SECTIONS, CLIPS, FRAMES, SIDE, SIDE, CH), 1.0, 6.0, ((0, 2), (1, 16))),
        "cotangent": normal_values(keys[1], (CLIPS, FRAMES, SIDE, SIDE, REGIONS), 1.0, 6.0, ((0, 16),)),
        "sessions": set_ends(jax.random.randint(keys[2], (CLIPS,), 0, SESSIONS), jax.random.fold_in(keys[2], 1), 0, SESSIONS - 1).astype(jnp.int32),
        "point_weight": normal_values(keys[3], (SECTIONS, CH, CH), CH ** -0.5, 0.21875, ((0, 2), (1, 16))),
        "spatial_kernel": normal_values(keys[4], (SECTIONS, 9, CH), 0.3, 1.5, ((0, 2),), jnp.float32),
        "temporal_kernel": normal_values(keys[5], (SECTIONS, TAPS, CH), 0.4, 2.0, ((0, 2),), jnp.float32),
        "readout": normal_values(keys[6], (SESSIONS, REGIONS, CH), REGIONS ** -0.5, 0.5),
    }


INV_ROOT_TWO = 0.7071067811865476
INV_ROOT_TAU = 0.3989422804014327

def gelu_value(pre_act):
    return 0.5 * pre_act * (1.0 + jax.scipy.special.erf(pre_act * INV_ROOT_TWO))

def gelu_slope(pre_act):
    return 0.5 * (1.0 + jax.scipy.special.erf(pre_act * INV_ROOT_TWO)) + pre_act * jnp.exp(-0.5 * pre_act * pre_act) * INV_ROOT_TAU

def spatial_pad(field_in):
    pad_spec = [(0, 0)] * (field_in.ndim - 3) + [(1, 1), (1, 1), (0, 0)]
    return jnp.pad(field_in, pad_spec)

def spatial(field_in, kernel):
    height, width = (field_in.shape[-3], field_in.shape[-2])
    padded = spatial_pad(field_in)
    summed = jnp.zeros_like(field_in)
    for row_off in range(3):
        for col_off in range(3):
            summed = summed + kernel[3 * row_off + col_off] * padded[..., row_off:row_off + height, col_off:col_off + width, :]
    return summed

def spatial_back(grad_in, kernel):
    height, width = (grad_in.shape[-3], grad_in.shape[-2])
    padded = spatial_pad(grad_in)
    summed = jnp.zeros_like(grad_in)
    for row_off in range(3):
        for col_off in range(3):
            summed = summed + kernel[3 * row_off + col_off] * padded[..., 2 - row_off:2 - row_off + height, 2 - col_off:2 - col_off + width, :]
    return summed

def spatial_kernel_grad(field_in, grad_in):
    height, width = (field_in.shape[-3], field_in.shape[-2])
    padded = spatial_pad(field_in)
    axes_all = tuple(range(field_in.ndim - 1))
    parts = []
    for row_off in range(3):
        for col_off in range(3):
            parts.append(lax.optimization_barrier(jnp.sum(padded[..., row_off:row_off + height, col_off:col_off + width, :] * grad_in, axis=axes_all)))
    return jnp.stack(parts)

def front_pad(field_in, tap_count):
    pad_spec = [(0, 0)] * (field_in.ndim - 4) + [(tap_count - 1, 0), (0, 0), (0, 0), (0, 0)]
    return jnp.pad(field_in, pad_spec)

def temporal(field_in, kernel):
    tap_count = kernel.shape[0]
    frames = field_in.shape[-4]
    padded = front_pad(field_in, tap_count)
    summed = jnp.zeros_like(field_in)
    for delay in range(tap_count):
        first = tap_count - 1 - delay
        summed = summed + kernel[delay] * padded[..., first:first + frames, :, :, :]
    return summed

def temporal_back(grad_in, kernel):
    tap_count = kernel.shape[0]
    frames = grad_in.shape[-4]
    pad_spec = [(0, 0)] * (grad_in.ndim - 4) + [(0, tap_count - 1), (0, 0), (0, 0), (0, 0)]
    padded = jnp.pad(grad_in, pad_spec)
    summed = jnp.zeros_like(grad_in)
    for delay in range(tap_count):
        summed = summed + kernel[delay] * padded[..., delay:delay + frames, :, :, :]
    return summed

def temporal_kernel_grad(field_in, grad_in, tap_count):
    frames = field_in.shape[-4]
    padded = front_pad(field_in, tap_count)
    axes_all = tuple(range(field_in.ndim - 1))
    parts = []
    for delay in range(tap_count):
        first = tap_count - 1 - delay
        parts.append(lax.optimization_barrier(jnp.sum(padded[..., first:first + frames, :, :, :] * grad_in, axis=axes_all)))
    return jnp.stack(parts)

def section_back(inputs, grad_out, s_kernel, t_kernel, weight):
    field_in = inputs.astype(jnp.float32)
    spread = spatial(field_in, s_kernel)
    pre_act = temporal(spread, t_kernel)
    hidden = gelu_value(pre_act).astype(jnp.bfloat16)
    channels = weight.shape[1]
    flat_grad = grad_out.reshape(-1, channels)
    flat_hidden = hidden.reshape(-1, channels)
    hidden_grad = jnp.dot(flat_grad, weight.T, preferred_element_type=jnp.float32).reshape(pre_act.shape)
    pre_grad = hidden_grad * gelu_slope(pre_act)
    spread_grad = temporal_back(pre_grad, t_kernel)
    in_grad = (grad_out.astype(jnp.float32) + spatial_back(spread_grad, s_kernel)).astype(jnp.bfloat16)
    weight_grad = jnp.dot(flat_hidden.T, flat_grad, preferred_element_type=jnp.float32)
    s_part = spatial_kernel_grad(field_in, spread_grad)
    t_part = temporal_kernel_grad(spread, pre_grad, t_kernel.shape[0])
    return (in_grad, weight_grad, s_part, t_part)

def reference(section_inputs, cotangent, sessions, point_weight, spatial_kernel, temporal_kernel, readout):
    chosen = jnp.take(readout, sessions, axis=0)
    grad_now = jnp.einsum('cfhwr,crk->cfhwk', cotangent.astype(jnp.float32), chosen.astype(jnp.float32)).astype(jnp.bfloat16)
    factor = 1.0 / math.sqrt(CLIPS * FRAMES * SIDE * SIDE)
    point_list, spatial_list, temporal_list = ([], [], [])
    for section_id in reversed(range(SECTIONS)):
        s_kernel = spatial_kernel[section_id]
        t_kernel = temporal_kernel[section_id]
        weight = point_weight[section_id]

        def scan_step(grad_sums, scan_item):
            inputs, grad_out = scan_item
            in_grad, w_part, s_part, t_part = section_back(inputs[None], grad_out[None], s_kernel, t_kernel, weight)
            return ((grad_sums[0] + w_part, grad_sums[1] + s_part, grad_sums[2] + t_part), in_grad[0])
        zero_sums = (jnp.zeros((CH, CH), jnp.float32), jnp.zeros((9, CH), jnp.float32), jnp.zeros((TAPS, CH), jnp.float32))
        grad_sums, grad_now = lax.scan(scan_step, zero_sums, (section_inputs[section_id], grad_now))
        point_list.append(grad_sums[0] * factor)
        spatial_list.append(grad_sums[1] * factor)
        temporal_list.append(grad_sums[2] * factor)
    return (jnp.stack(point_list[::-1]), jnp.stack(spatial_list[::-1]), jnp.stack(temporal_list[::-1]))
```

```python
import functools
import math

import jax
import jax.numpy as jnp
from jax import lax
from jax.experimental import pallas as pl
from jax.experimental.pallas import tpu as pltpu
from jax.sharding import PartitionSpec as P

INV_ROOT_TWO = 0.7071067811865476
INV_ROOT_TAU = 0.3989422804014327
LANES = 128


def from_behind(block, axis, distance):
    devices = range(lax.axis_size(axis))
    route = [(i - distance, i) for i in devices if i - distance in devices]
    return lax.ppermute(block, axis, route)


def gelu_value(pre_act):
    return 0.5 * pre_act * (1.0 + jax.scipy.special.erf(pre_act * INV_ROOT_TWO))


def gelu_slope(pre_act):
    return (
        0.5 * (1.0 + jax.scipy.special.erf(pre_act * INV_ROOT_TWO))
        + pre_act * jnp.exp(-0.5 * pre_act * pre_act) * INV_ROOT_TAU
    )


def spatial_pad(field_in):
    pad_spec = [(0, 0)] * (field_in.ndim - 3) + [(1, 1), (1, 1), (0, 0)]
    return jnp.pad(field_in, pad_spec)


def spatial(field_in, kernel):
    height, width = (field_in.shape[-3], field_in.shape[-2])
    padded = spatial_pad(field_in)
    summed = jnp.zeros_like(field_in)
    for row_off in range(3):
        for col_off in range(3):
            summed = (
                summed
                + kernel[3 * row_off + col_off]
                * padded[..., row_off : row_off + height, col_off : col_off + width, :]
            )
    return summed


def spatial_back(grad_in, kernel):
    height, width = (grad_in.shape[-3], grad_in.shape[-2])
    padded = spatial_pad(grad_in)
    summed = jnp.zeros_like(grad_in)
    for row_off in range(3):
        for col_off in range(3):
            summed = (
                summed
                + kernel[3 * row_off + col_off]
                * padded[
                    ..., 2 - row_off : 2 - row_off + height, 2 - col_off : 2 - col_off + width, :
                ]
            )
    return summed


def spatial_kernel_grad(field_in, grad_in):
    height, width = (field_in.shape[-3], field_in.shape[-2])
    padded = spatial_pad(field_in)
    axes_all = tuple(range(field_in.ndim - 1))
    parts = []
    for row_off in range(3):
        for col_off in range(3):
            parts.append(
                jnp.sum(
                    padded[..., row_off : row_off + height, col_off : col_off + width, :] * grad_in,
                    axis=axes_all,
                )
            )
    return jnp.stack(parts)


def front_pad(field_in, tap_count):
    pad_spec = [(0, 0)] * (field_in.ndim - 4) + [(tap_count - 1, 0), (0, 0), (0, 0), (0, 0)]
    return jnp.pad(field_in, pad_spec)


def temporal(field_in, kernel):
    tap_count = kernel.shape[0]
    frames = field_in.shape[-4]
    padded = front_pad(field_in, tap_count)
    summed = jnp.zeros_like(field_in)
    for delay in range(tap_count):
        first = tap_count - 1 - delay
        summed = summed + kernel[delay] * padded[..., first : first + frames, :, :, :]
    return summed


def temporal_back(grad_in, kernel):
    tap_count = kernel.shape[0]
    frames = grad_in.shape[-4]
    pad_spec = [(0, 0)] * (grad_in.ndim - 4) + [(0, tap_count - 1), (0, 0), (0, 0), (0, 0)]
    padded = jnp.pad(grad_in, pad_spec)
    summed = jnp.zeros_like(grad_in)
    for delay in range(tap_count):
        summed = summed + kernel[delay] * padded[..., delay : delay + frames, :, :, :]
    return summed


def temporal_kernel_grad(field_in, grad_in, tap_count):
    frames = field_in.shape[-4]
    padded = front_pad(field_in, tap_count)
    axes_all = tuple(range(field_in.ndim - 1))
    parts = []
    for delay in range(tap_count):
        first = tap_count - 1 - delay
        parts.append(jnp.sum(padded[..., first : first + frames, :, :, :] * grad_in, axis=axes_all))
    return jnp.stack(parts)


def section_back(inputs, grad_out, s_kernel, t_kernel, hidden_of):
    field_in = inputs.astype(jnp.float32)
    spread = spatial(field_in, s_kernel)
    pre_act = temporal(spread, t_kernel)
    hidden = gelu_value(pre_act).astype(jnp.bfloat16)
    channels = inputs.shape[-1]
    flat_grad = grad_out.reshape(-1, channels)
    flat_hidden = hidden.reshape(-1, channels)
    hidden_grad = hidden_of(flat_grad).reshape(pre_act.shape)
    pre_grad = hidden_grad * gelu_slope(pre_act)
    spread_grad = temporal_back(pre_grad, t_kernel)
    in_grad = (grad_out.astype(jnp.float32) + spatial_back(spread_grad, s_kernel)).astype(
        jnp.bfloat16
    )
    weight_grad = jnp.dot(flat_hidden.T, flat_grad, preferred_element_type=jnp.float32)
    s_part = spatial_kernel_grad(field_in, spread_grad)
    t_part = temporal_kernel_grad(spread, pre_grad, t_kernel.shape[0])
    return (in_grad, weight_grad, s_part, t_part)


def pipelined(
    section_inputs, cotangent, sessions, point_weight, spatial_kernel, temporal_kernel, readout
):
    section_count = lax.axis_size("section")
    my_section = lax.axis_index("section")
    inputs = section_inputs[0]
    s_kernel = spatial_kernel[0]
    t_kernel = temporal_kernel[0]
    weight_shard = point_weight[0]
    clip_count = inputs.shape[0]
    channels = inputs.shape[-1]
    chosen = jnp.take(readout, sessions, axis=0)
    top_grads = jnp.einsum(
        "cfhwr,crk->cfhwk", cotangent, chosen, preferred_element_type=jnp.float32
    ).astype(jnp.bfloat16)
    block_size = 2
    step_count = clip_count // block_size
    tick_count = step_count + section_count - 1
    full_weight = lax.all_gather(weight_shard, "dp", axis=0, tiled=True)

    def hidden_of(flat_grad):
        return jnp.dot(flat_grad, full_weight.T, preferred_element_type=jnp.float32)

    block_shape = (block_size,) + inputs.shape[1:]

    def tick(tick_index, state_now):
        incoming, w_sum, s_sum, t_sum = state_now
        clip_step = tick_index - (section_count - 1 - my_section)
        is_live = (clip_step >= 0) & (clip_step < step_count)
        first_clip = jnp.clip(clip_step, 0, step_count - 1) * block_size
        inputs_block = lax.dynamic_slice_in_dim(inputs, first_clip, block_size, 0)
        top_block = lax.dynamic_slice_in_dim(top_grads, first_clip, block_size, 0)
        grad_out = jnp.where(my_section == section_count - 1, top_block, incoming)

        def live_work(sums):
            in_grad, w_part, s_part, t_part = section_back(
                inputs_block, grad_out, s_kernel, t_kernel, hidden_of
            )
            return (in_grad, sums[0] + w_part, sums[1] + s_part, sums[2] + t_part)

        def dead_work(sums):
            return (jnp.zeros(block_shape, jnp.bfloat16), sums[0], sums[1], sums[2])

        in_grad, w_new, s_new, t_new = lax.cond(
            is_live, live_work, dead_work, (w_sum, s_sum, t_sum)
        )
        passed = from_behind(in_grad, "section", -1)
        return (passed, w_new, s_new, t_new)

    start_state = (
        jnp.zeros(block_shape, jnp.bfloat16),
        jnp.zeros((channels, channels), jnp.float32),
        jnp.zeros((9, channels), jnp.float32),
        jnp.zeros(t_kernel.shape, jnp.float32),
    )
    finals = lax.fori_loop(0, tick_count, tick, start_state)
    weight_grads = lax.psum_scatter(finals[1], "dp", scatter_dimension=0, tiled=True)
    s_total, t_total = lax.psum((finals[2], finals[3]), "dp")
    rows_all = (
        clip_count * lax.axis_size("dp") * inputs.shape[1] * inputs.shape[2] * inputs.shape[3]
    )
    factor = 1.0 / math.sqrt(rows_all)
    return ((weight_grads * factor)[None], (s_total * factor)[None], (t_total * factor)[None])


def section_kernel(
    first, frames, side, sess_ref, x_ref, g_in_ref, read_ref, w_ref, sk_ref, tk_ref, *rest
):
    if first:
        ing_ref, wg_ref, st_ref, g_ref, hg_ref, hid_ref, acc_ref = rest
    else:
        wg_ref, st_ref, hg_ref, hid_ref, acc_ref = rest
        g_ref = g_in_ref
    cells = side * side
    clip_rows = cells * frames
    taps = tk_ref.shape[0]
    channels = w_ref.shape[1]
    rows = x_ref.shape[0]
    clips = rows // clip_rows
    if first:
        for clip in range(clips):
            span = pl.ds(clip * clip_rows, clip_rows)
            g_ref[span, :] = jnp.dot(
                g_in_ref[span, :], read_ref[sess_ref[clip]], preferred_element_type=jnp.float32
            ).astype(jnp.bfloat16)
    hg_ref[...] = lax.dot_general(
        g_ref[...], w_ref[...], (((1,), (1,)), ((), ())), preferred_element_type=jnp.float32
    )
    acc_ref[...] = jnp.zeros_like(acc_ref)
    frame_of = lax.broadcasted_iota(jnp.int32, (frames, LANES), 0)
    chunks = channels // LANES

    def step(index, carry):
        clip = index // chunks
        lanes = pl.ds(pl.multiple_of((index % chunks) * LANES, LANES), LANES)
        span = pl.ds(pl.multiple_of(clip * clip_rows, clip_rows), clip_rows)

        def tile(value):
            return jnp.broadcast_to(value, (frames, LANES))

        s_taps = [tile(sk_ref[k : k + 1, lanes]) for k in range(9)]
        t_taps = [tile(tk_ref[d : d + 1, lanes]) for d in range(taps)]
        t_front = [jnp.where(frame_of >= d, t_taps[d], 0.0) for d in range(taps)]
        t_tail = [jnp.where(frame_of < frames - d, t_taps[d], 0.0) for d in range(taps)]
        x_all = x_ref[span, lanes].astype(jnp.float32)
        hg_all = hg_ref[span, lanes]
        x = [x_all[c * frames : (c + 1) * frames] for c in range(cells)]
        inside = lambda i, j: 0 <= i < side and 0 <= j < side
        spread, sgrad, hidden = [], [], []
        t_sums = [None] * taps
        for i in range(side):
            for j in range(side):
                total = None
                for r in range(3):
                    for q in range(3):
                        if inside(i + r - 1, j + q - 1):
                            term = s_taps[3 * r + q] * x[(i + r - 1) * side + j + q - 1]
                            total = term if total is None else total + term
                pre = t_taps[0] * total
                for d in range(1, taps):
                    pre = pre + t_front[d] * pltpu.roll(total, d, 0)
                half = 0.5 + 0.5 * lax.erf(pre * INV_ROOT_TWO)
                hidden.append(pre * half)
                slope = half + pre * jnp.exp(-0.5 * pre * pre) * INV_ROOT_TAU
                c = i * side + j
                pgrad = hg_all[c * frames : (c + 1) * frames] * slope
                back = t_taps[0] * pgrad
                for d in range(taps):
                    moved = pgrad if d == 0 else pltpu.roll(pgrad, frames - d, 0)
                    if d:
                        back = back + t_tail[d] * moved
                    part = total * moved
                    t_sums[d] = part if t_sums[d] is None else t_sums[d] + part
                sgrad.append(back)
        hid_ref[span, lanes] = jnp.concatenate(hidden, axis=0).astype(jnp.bfloat16)
        for d in range(taps):
            acc_ref[9 + d, :, lanes] += t_sums[d]
        s_sums = [None] * 9
        for i in range(side):
            for j in range(side):
                for r in range(3):
                    for q in range(3):
                        if inside(i + r - 1, j + q - 1):
                            part = x[(i + r - 1) * side + j + q - 1] * sgrad[i * side + j]
                            k = 3 * r + q
                            s_sums[k] = part if s_sums[k] is None else s_sums[k] + part
        for k in range(9):
            acc_ref[k, :, lanes] += s_sums[k]
        if first:
            out = []
            for i in range(side):
                for j in range(side):
                    total = None
                    for r in range(3):
                        for q in range(3):
                            if inside(i - r + 1, j - q + 1):
                                term = s_taps[3 * r + q] * sgrad[(i - r + 1) * side + j - q + 1]
                                total = term if total is None else total + term
                    out.append(total)
            ing_ref[span, lanes] = (
                g_ref[span, lanes].astype(jnp.float32) + jnp.concatenate(out, axis=0)
            ).astype(jnp.bfloat16)
        return carry

    lax.fori_loop(0, clips * chunks, step, 0)
    wg_ref[...] = lax.dot_general(
        hid_ref[...], g_ref[...], (((0,), (0,)), ((), ())), preferred_element_type=jnp.float32
    ).astype(wg_ref.dtype)
    wide = lax.broadcasted_iota(jnp.int32, (frames, channels), 0)
    for k in range(9):
        st_ref[k : k + 1, :] = jnp.sum(acc_ref[k], axis=0, keepdims=True)
    for d in range(taps):
        kept = jnp.where(wide < frames - d, acc_ref[9 + d], 0.0)
        st_ref[9 + d : 10 + d, :] = jnp.sum(kept, axis=0, keepdims=True)


def section_call(first, frames, side, sess, x, g_in, read, weight, sk, tk):
    rows, channels = x.shape
    vmem = pl.BlockSpec(memory_space=pltpu.VMEM)
    out_shape = [
        jax.ShapeDtypeStruct((channels, channels), jnp.bfloat16),
        jax.ShapeDtypeStruct((9 + tk.shape[0], channels), jnp.float32),
    ]
    scratch = [
        pltpu.VMEM((rows, channels), jnp.float32),
        pltpu.VMEM((rows, channels), jnp.bfloat16),
        pltpu.VMEM((9 + tk.shape[0], frames, channels), jnp.float32),
    ]
    if first:
        out_shape = [jax.ShapeDtypeStruct((rows, channels), jnp.bfloat16)] + out_shape
        scratch = [pltpu.VMEM((rows, channels), jnp.bfloat16)] + scratch
    return pl.pallas_call(
        functools.partial(section_kernel, first, frames, side),
        out_shape=out_shape,
        in_specs=[pl.BlockSpec(memory_space=pltpu.SMEM)] + [vmem] * 6,
        out_specs=[vmem] * len(out_shape),
        scratch_shapes=scratch,
        compiler_params=pltpu.CompilerParams(vmem_limit_bytes=40 << 20),
        cost_estimate=pl.CostEstimate(
            flops=4 * rows * channels * channels, bytes_accessed=8 << 20, transcendentals=0
        ),
        name="section_first" if first else "section_next",
    )(sess, x, g_in, read, weight, sk, tk)


def dp_swap(block, mask):
    return lax.ppermute(block, "dp", [(i, i ^ mask) for i in range(16)])


def section_swap(block):
    return lax.ppermute(block, "section", [(0, 1), (1, 0)])


def pick(block, index, axis):
    return lax.dynamic_index_in_dim(block, index, axis, keepdims=False)


def local(
    section_inputs, cotangent, sessions, point_weight, spatial_kernel, temporal_kernel, readout
):
    mine = lax.axis_index("section")
    dp_index = lax.axis_index("dp")
    _, clip_count, frames, side, _, channels = section_inputs.shape
    cells = side * side
    part = clip_count // 2
    f32 = jnp.float32

    def by_cell(block):
        last = block.shape[-1]
        return block.reshape(-1, frames, cells, last).transpose(0, 2, 1, 3).reshape(-1, last)

    away = lax.dynamic_slice_in_dim(section_inputs[0], (1 - mine) * part, part, 0)
    kept = lax.dynamic_slice_in_dim(section_inputs[0], mine * part, part, 0)
    came = section_swap(by_cell(away))
    kept = by_cell(kept)
    x_top = jnp.where(mine == 1, kept, came)
    x_low = jnp.where(mine == 1, came, kept)
    cot = by_cell(lax.dynamic_slice_in_dim(cotangent, mine * part, part, 0))
    sess = lax.dynamic_slice_in_dim(sessions, mine * part, part, 0)
    weights = lax.all_gather(point_weight[0], ("section", "dp"), axis=0, tiled=True)
    w_low, w_top = weights[:channels], weights[channels:]
    kernels = jnp.concatenate([spatial_kernel[0], temporal_kernel[0]], axis=0)
    kernels_other = section_swap(kernels)
    k_top = jnp.where(mine == 1, kernels, kernels_other)
    k_low = jnp.where(mine == 1, kernels_other, kernels)

    in_grad, wg_top, st_top = section_call(
        True, frames, side, sess, x_top, cot, readout, w_top, k_top[:9], k_top[9:]
    )
    wg_low, st_low = section_call(
        False, frames, side, sess, x_low, in_grad, readout, w_low, k_low[:9], k_low[9:]
    )

    core = dp_index % 2
    x_at = (dp_index // 2) % 2
    z_at = dp_index // 4
    bf16 = jnp.bfloat16

    def core_stage(wg):
        split = wg.reshape(4, 2, 2, channels // 16, channels)
        got = dp_swap(pick(split, 1 - core, 2), 1)
        return pick(split, core, 2).astype(f32) + got.astype(f32)

    top_sum = core_stage(wg_top)
    low_sum = core_stage(wg_low)
    stacked_send = jnp.where(mine == 1, low_sum, top_sum).astype(bf16)
    own = jnp.where(mine == 1, top_sum, low_sum)
    own = own + section_swap(stacked_send).astype(f32)
    got = dp_swap(pick(own, 1 - x_at, 1).astype(bf16), 2)
    own = pick(own, x_at, 1) + got.astype(f32)
    total = pick(own, z_at, 0)
    narrow = own.astype(bf16)
    for hop in range(1, 4):
        route = [(i, (i + 4 * hop) % 16) for i in range(16)]
        total = total + lax.ppermute(pick(narrow, (z_at + hop) % 4, 0), "dp", route).astype(f32)

    st_send = jnp.where(mine == 1, st_low, st_top)
    st_own = jnp.where(mine == 1, st_top, st_low) + section_swap(st_send)
    for mask in (1, 2, 4, 8):
        st_own = st_own + dp_swap(st_own, mask)
    factor = 1.0 / math.sqrt(clip_count * lax.axis_size("dp") * frames * cells)
    st_own = st_own * factor
    return ((total * factor)[None], st_own[:9][None], st_own[9:][None])


def solution(mesh):
    halves = mesh.shape["section"] == 2 and mesh.shape["dp"] == 16
    return jax.shard_map(
        local if halves else pipelined,
        mesh=mesh,
        in_specs=(
            P("section", "dp", None, None, None, None),
            P("dp", None, None, None, None),
            P("dp"),
            P("section", "dp", None),
            P("section", None, None),
            P("section", None, None),
            P(),
        ),
        out_specs=(P("section", "dp", None), P("section", None, None), P("section", None, None)),
        check_vma=False,
    )
```

```python
import functools
import math

import jax
import jax.numpy as jnp
from jax import lax
from jax.experimental import pallas as pl
from jax.experimental.pallas import tpu as pltpu
from jax.sharding import PartitionSpec as P

INV_ROOT_TWO = 0.7071067811865476
INV_ROOT_TAU = 0.3989422804014327
LANES = 128
MESH = pl.DeviceIdType.MESH


def from_behind(block, axis, distance):
    devices = range(lax.axis_size(axis))
    route = [(i - distance, i) for i in devices if i - distance in devices]
    return lax.ppermute(block, axis, route)


def gelu_value(pre_act):
    return 0.5 * pre_act * (1.0 + jax.scipy.special.erf(pre_act * INV_ROOT_TWO))


def gelu_slope(pre_act):
    return (
        0.5 * (1.0 + jax.scipy.special.erf(pre_act * INV_ROOT_TWO))
        + pre_act * jnp.exp(-0.5 * pre_act * pre_act) * INV_ROOT_TAU
    )


def spatial_pad(field_in):
    pad_spec = [(0, 0)] * (field_in.ndim - 3) + [(1, 1), (1, 1), (0, 0)]
    return jnp.pad(field_in, pad_spec)


def spatial(field_in, kernel):
    height, width = (field_in.shape[-3], field_in.shape[-2])
    padded = spatial_pad(field_in)
    summed = jnp.zeros_like(field_in)
    for row_off in range(3):
        for col_off in range(3):
            summed = (
                summed
                + kernel[3 * row_off + col_off]
                * padded[..., row_off : row_off + height, col_off : col_off + width, :]
            )
    return summed


def spatial_back(grad_in, kernel):
    height, width = (grad_in.shape[-3], grad_in.shape[-2])
    padded = spatial_pad(grad_in)
    summed = jnp.zeros_like(grad_in)
    for row_off in range(3):
        for col_off in range(3):
            summed = (
                summed
                + kernel[3 * row_off + col_off]
                * padded[
                    ..., 2 - row_off : 2 - row_off + height, 2 - col_off : 2 - col_off + width, :
                ]
            )
    return summed


def spatial_kernel_grad(field_in, grad_in):
    height, width = (field_in.shape[-3], field_in.shape[-2])
    padded = spatial_pad(field_in)
    axes_all = tuple(range(field_in.ndim - 1))
    parts = []
    for row_off in range(3):
        for col_off in range(3):
            parts.append(
                jnp.sum(
                    padded[..., row_off : row_off + height, col_off : col_off + width, :] * grad_in,
                    axis=axes_all,
                )
            )
    return jnp.stack(parts)


def front_pad(field_in, tap_count):
    pad_spec = [(0, 0)] * (field_in.ndim - 4) + [(tap_count - 1, 0), (0, 0), (0, 0), (0, 0)]
    return jnp.pad(field_in, pad_spec)


def temporal(field_in, kernel):
    tap_count = kernel.shape[0]
    frames = field_in.shape[-4]
    padded = front_pad(field_in, tap_count)
    summed = jnp.zeros_like(field_in)
    for delay in range(tap_count):
        first = tap_count - 1 - delay
        summed = summed + kernel[delay] * padded[..., first : first + frames, :, :, :]
    return summed


def temporal_back(grad_in, kernel):
    tap_count = kernel.shape[0]
    frames = grad_in.shape[-4]
    pad_spec = [(0, 0)] * (grad_in.ndim - 4) + [(0, tap_count - 1), (0, 0), (0, 0), (0, 0)]
    padded = jnp.pad(grad_in, pad_spec)
    summed = jnp.zeros_like(grad_in)
    for delay in range(tap_count):
        summed = summed + kernel[delay] * padded[..., delay : delay + frames, :, :, :]
    return summed


def temporal_kernel_grad(field_in, grad_in, tap_count):
    frames = field_in.shape[-4]
    padded = front_pad(field_in, tap_count)
    axes_all = tuple(range(field_in.ndim - 1))
    parts = []
    for delay in range(tap_count):
        first = tap_count - 1 - delay
        parts.append(jnp.sum(padded[..., first : first + frames, :, :, :] * grad_in, axis=axes_all))
    return jnp.stack(parts)


def section_back(inputs, grad_out, s_kernel, t_kernel, hidden_of):
    field_in = inputs.astype(jnp.float32)
    spread = spatial(field_in, s_kernel)
    pre_act = temporal(spread, t_kernel)
    hidden = gelu_value(pre_act).astype(jnp.bfloat16)
    channels = inputs.shape[-1]
    flat_grad = grad_out.reshape(-1, channels)
    flat_hidden = hidden.reshape(-1, channels)
    hidden_grad = hidden_of(flat_grad).reshape(pre_act.shape)
    pre_grad = hidden_grad * gelu_slope(pre_act)
    spread_grad = temporal_back(pre_grad, t_kernel)
    in_grad = (grad_out.astype(jnp.float32) + spatial_back(spread_grad, s_kernel)).astype(
        jnp.bfloat16
    )
    weight_grad = jnp.dot(flat_hidden.T, flat_grad, preferred_element_type=jnp.float32)
    s_part = spatial_kernel_grad(field_in, spread_grad)
    t_part = temporal_kernel_grad(spread, pre_grad, t_kernel.shape[0])
    return (in_grad, weight_grad, s_part, t_part)


def pipelined(
    section_inputs, cotangent, sessions, point_weight, spatial_kernel, temporal_kernel, readout
):
    section_count = lax.axis_size("section")
    my_section = lax.axis_index("section")
    inputs = section_inputs[0]
    s_kernel = spatial_kernel[0]
    t_kernel = temporal_kernel[0]
    weight_shard = point_weight[0]
    clip_count = inputs.shape[0]
    channels = inputs.shape[-1]
    chosen = jnp.take(readout, sessions, axis=0)
    top_grads = jnp.einsum(
        "cfhwr,crk->cfhwk", cotangent, chosen, preferred_element_type=jnp.float32
    ).astype(jnp.bfloat16)
    block_size = 2
    step_count = clip_count // block_size
    tick_count = step_count + section_count - 1
    full_weight = lax.all_gather(weight_shard, "dp", axis=0, tiled=True)

    def hidden_of(flat_grad):
        return jnp.dot(flat_grad, full_weight.T, preferred_element_type=jnp.float32)

    block_shape = (block_size,) + inputs.shape[1:]

    def tick(tick_index, state_now):
        incoming, w_sum, s_sum, t_sum = state_now
        clip_step = tick_index - (section_count - 1 - my_section)
        is_live = (clip_step >= 0) & (clip_step < step_count)
        first_clip = jnp.clip(clip_step, 0, step_count - 1) * block_size
        inputs_block = lax.dynamic_slice_in_dim(inputs, first_clip, block_size, 0)
        top_block = lax.dynamic_slice_in_dim(top_grads, first_clip, block_size, 0)
        grad_out = jnp.where(my_section == section_count - 1, top_block, incoming)

        def live_work(sums):
            in_grad, w_part, s_part, t_part = section_back(
                inputs_block, grad_out, s_kernel, t_kernel, hidden_of
            )
            return (in_grad, sums[0] + w_part, sums[1] + s_part, sums[2] + t_part)

        def dead_work(sums):
            return (jnp.zeros(block_shape, jnp.bfloat16), sums[0], sums[1], sums[2])

        in_grad, w_new, s_new, t_new = lax.cond(
            is_live, live_work, dead_work, (w_sum, s_sum, t_sum)
        )
        passed = from_behind(in_grad, "section", -1)
        return (passed, w_new, s_new, t_new)

    start_state = (
        jnp.zeros(block_shape, jnp.bfloat16),
        jnp.zeros((channels, channels), jnp.float32),
        jnp.zeros((9, channels), jnp.float32),
        jnp.zeros(t_kernel.shape, jnp.float32),
    )
    finals = lax.fori_loop(0, tick_count, tick, start_state)
    weight_grads = lax.psum_scatter(finals[1], "dp", scatter_dimension=0, tiled=True)
    s_total, t_total = lax.psum((finals[2], finals[3]), "dp")
    rows_all = (
        clip_count * lax.axis_size("dp") * inputs.shape[1] * inputs.shape[2] * inputs.shape[3]
    )
    factor = 1.0 / math.sqrt(rows_all)
    return ((weight_grads * factor)[None], (s_total * factor)[None], (t_total * factor)[None])


def section_work(
    first, frames, side, sess_ref, x_ref, g_in_ref, read_ref, w_ref, k_ref, taps, wg_ref, st_ref,
    ing_ref, g_ref, hg_ref, hid_ref, acc_ref
):
    cells = side * side
    clip_rows = cells * frames
    channels = w_ref.shape[1]
    rows = x_ref.shape[0]
    clips = rows // clip_rows
    if first:
        for clip in range(clips):
            span = pl.ds(clip * clip_rows, clip_rows)
            g_ref[span, :] = jnp.dot(
                g_in_ref[span, :], read_ref[sess_ref[clip]], preferred_element_type=jnp.float32
            ).astype(jnp.bfloat16)
    hg_ref[...] = lax.dot_general(
        g_ref[...], w_ref[...], (((1,), (1,)), ((), ())), preferred_element_type=jnp.float32
    )
    acc_ref[...] = jnp.zeros_like(acc_ref)
    frame_of = lax.broadcasted_iota(jnp.int32, (frames, LANES), 0)
    chunks = channels // LANES

    def step(index, carry):
        clip = index // chunks
        lanes = pl.ds(pl.multiple_of((index % chunks) * LANES, LANES), LANES)
        span = pl.ds(pl.multiple_of(clip * clip_rows, clip_rows), clip_rows)

        def tile(value):
            return jnp.broadcast_to(value, (frames, LANES))

        s_taps = [tile(k_ref[k : k + 1, lanes]) for k in range(9)]
        t_taps = [tile(k_ref[9 + d : 10 + d, lanes]) for d in range(taps)]
        t_front = [jnp.where(frame_of >= d, t_taps[d], 0.0) for d in range(taps)]
        t_tail = [jnp.where(frame_of < frames - d, t_taps[d], 0.0) for d in range(taps)]
        x_all = x_ref[span, lanes].astype(jnp.float32)
        hg_all = hg_ref[span, lanes]
        x = [x_all[c * frames : (c + 1) * frames] for c in range(cells)]
        inside = lambda i, j: 0 <= i < side and 0 <= j < side
        spread, sgrad, hidden = [], [], []
        t_sums = [None] * taps
        for i in range(side):
            for j in range(side):
                total = None
                for r in range(3):
                    for q in range(3):
                        if inside(i + r - 1, j + q - 1):
                            term = s_taps[3 * r + q] * x[(i + r - 1) * side + j + q - 1]
                            total = term if total is None else total + term
                pre = t_taps[0] * total
                for d in range(1, taps):
                    pre = pre + t_front[d] * pltpu.roll(total, d, 0)
                half = 0.5 + 0.5 * lax.erf(pre * INV_ROOT_TWO)
                hidden.append(pre * half)
                slope = half + pre * jnp.exp(-0.5 * pre * pre) * INV_ROOT_TAU
                c = i * side + j
                pgrad = hg_all[c * frames : (c + 1) * frames] * slope
                back = t_taps[0] * pgrad
                for d in range(taps):
                    moved = pgrad if d == 0 else pltpu.roll(pgrad, frames - d, 0)
                    if d:
                        back = back + t_tail[d] * moved
                    part = total * moved
                    t_sums[d] = part if t_sums[d] is None else t_sums[d] + part
                sgrad.append(back)
        hid_ref[span, lanes] = jnp.concatenate(hidden, axis=0).astype(jnp.bfloat16)
        for d in range(taps):
            acc_ref[9 + d, :, lanes] += t_sums[d]
        s_sums = [None] * 9
        for i in range(side):
            for j in range(side):
                for r in range(3):
                    for q in range(3):
                        if inside(i + r - 1, j + q - 1):
                            part = x[(i + r - 1) * side + j + q - 1] * sgrad[i * side + j]
                            k = 3 * r + q
                            s_sums[k] = part if s_sums[k] is None else s_sums[k] + part
        for k in range(9):
            acc_ref[k, :, lanes] += s_sums[k]
        if first:
            out = []
            for i in range(side):
                for j in range(side):
                    total = None
                    for r in range(3):
                        for q in range(3):
                            if inside(i - r + 1, j - q + 1):
                                term = s_taps[3 * r + q] * sgrad[(i - r + 1) * side + j - q + 1]
                                total = term if total is None else total + term
                    out.append(total)
            ing_ref[span, lanes] = (
                g_ref[span, lanes].astype(jnp.float32) + jnp.concatenate(out, axis=0)
            ).astype(jnp.bfloat16)
        return carry

    lax.fori_loop(0, clips * chunks, step, 0)
    wg_ref[...] = lax.dot_general(
        hid_ref[...], g_ref[...], (((0,), (0,)), ((), ())), preferred_element_type=jnp.float32
    ).astype(wg_ref.dtype)
    wide = lax.broadcasted_iota(jnp.int32, (frames, channels), 0)
    st_ref[...] = jnp.zeros_like(st_ref)
    for k in range(9):
        st_ref[k : k + 1, :] = jnp.sum(acc_ref[k], axis=0, keepdims=True)
    for d in range(taps):
        kept = jnp.where(wide < frames - d, acc_ref[9 + d], 0.0)
        st_ref[9 + d : 10 + d, :] = jnp.sum(kept, axis=0, keepdims=True)


def both_kernel(
    frames, side, taps, sess_ref, x_ref, cot_ref, read_ref, w_ref, k_ref, wg_ref, st_ref, *scratch
):
    ing_ref, g_ref, hg_ref, hid_ref, acc_ref = scratch
    for sec in (1, 0):
        section_work(
            sec == 1,
            frames,
            side,
            sess_ref,
            x_ref.at[sec],
            cot_ref,
            read_ref,
            w_ref.at[sec],
            k_ref.at[sec],
            taps,
            wg_ref.at[sec],
            st_ref.at[sec],
            ing_ref,
            g_ref if sec == 1 else ing_ref,
            hg_ref,
            hid_ref,
            acc_ref,
        )


def both_call(frames, side, taps, sess, x, cot, read, weights, kernels):
    _, rows, channels = x.shape
    vmem = pl.BlockSpec(memory_space=pltpu.VMEM)
    return pl.pallas_call(
        functools.partial(both_kernel, frames, side, taps),
        out_shape=[
            jax.ShapeDtypeStruct((2, channels, channels), jnp.bfloat16),
            jax.ShapeDtypeStruct((2, 16, channels), jnp.float32),
        ],
        in_specs=[pl.BlockSpec(memory_space=pltpu.SMEM)] + [vmem] * 5,
        out_specs=[vmem] * 2,
        scratch_shapes=[
            pltpu.VMEM((rows, channels), jnp.bfloat16),
            pltpu.VMEM((rows, channels), jnp.bfloat16),
            pltpu.VMEM((rows, channels), jnp.float32),
            pltpu.VMEM((rows, channels), jnp.bfloat16),
            pltpu.VMEM((9 + taps, frames, channels), jnp.float32),
        ],
        compiler_params=pltpu.CompilerParams(vmem_limit_bytes=40 << 20),
        name="both_sections",
    )(sess, x, cot, read, weights, kernels)


def places():
    dp = lax.axis_index("dp")
    sec = lax.axis_index("section")
    return dp, sec, dp // 4, (dp // 2) % 2, dp % 2


def greet(partners):
    barrier = pltpu.get_barrier_semaphore()
    for there in partners:
        pl.semaphore_signal(barrier, inc=1, device_id=there, device_id_type=MESH)
    pl.semaphore_wait(barrier, len(partners))


def remote(src, dst, sems, slot, there):
    return pltpu.make_async_remote_copy(
        src_ref=src,
        dst_ref=dst,
        send_sem=sems[0].at[slot],
        recv_sem=sems[1].at[slot],
        device_id=there,
        device_id_type=MESH,
    )


def gather_kernel(
    x_ref, w_ref, k_ref, xo_ref, wo_ref, ko_ref, ys, yr, zs, zr, xs, xr, cs, cr, own_sem
):
    dp, sec, z, x, c = places()
    over = (dp, 1 - sec)
    mate = (z * 4 + x * 2 + 1 - c, sec)
    side_chip = (z * 4 + (1 - x) * 2 + c, sec)
    line = [((z + h) % 4 * 4 + x * 2 + c, sec) for h in (1, 2, 3)]
    greet([over, mate, side_chip] + line)
    secs = (sec, 1 - sec)
    sends = []

    def go(src, dst, sems, slot, there):
        copy = remote(src, dst, sems, slot, there)
        copy.start()
        sends.append(copy)
        return copy

    slot_of = wo_ref.at[sec, dp]
    y_w = go(w_ref, slot_of, (ys, yr), 0, over)
    y_k = go(k_ref, ko_ref.at[sec], (ys, yr), 1, over)
    y_x = go(x_ref.at[1 - sec], xo_ref.at[sec], (ys, yr), 2, over)
    z_w = {}
    x_w = {}
    c_w = {}
    for h in range(3):
        z_w[0, h] = go(w_ref, slot_of, (zs, zr), h, line[h])
    x_w[0, 0] = go(w_ref, slot_of, (xs, xr), 0, side_chip)
    c_w[0, 0] = go(w_ref, slot_of, (cs, cr), 0, mate)
    kept = [
        pltpu.make_async_copy(w_ref, slot_of, own_sem.at[0]),
        pltpu.make_async_copy(k_ref, ko_ref.at[sec], own_sem.at[1]),
        pltpu.make_async_copy(x_ref.at[sec], xo_ref.at[sec], own_sem.at[2]),
    ]
    for copy in kept:
        copy.start()
    y_w.wait_recv()
    held = wo_ref.at[1 - sec, dp]
    for h in range(3):
        z_w[1, h] = go(held, held, (zs, zr), 3 + h, line[h])
    x_w[1, 0] = go(held, held, (xs, xr), 4, side_chip)
    c_w[1, 0] = go(held, held, (cs, cr), 8, mate)
    for h in range(3):
        source = (z + 3 - h) % 4 * 4 + x * 2 + c
        for kind in range(2):
            z_w[kind, h].wait_recv()
            held = wo_ref.at[secs[kind], source]
            x_w[kind, h + 1] = go(held, held, (xs, xr), 4 * kind + h + 1, side_chip)
            c_w[kind, h + 1] = go(held, held, (cs, cr), 8 * kind + h + 1, mate)
    for h in range(4):
        source = (z + 4 - h) % 4 * 4 + (1 - x) * 2 + c
        for kind in range(2):
            x_w[kind, h].wait_recv()
            held = wo_ref.at[secs[kind], source]
            c_w[kind, h + 4] = go(held, held, (cs, cr), 8 * kind + h + 4, mate)
    for copy in c_w.values():
        copy.wait_recv()
    y_k.wait_recv()
    y_x.wait_recv()
    for copy in sends:
        copy.wait_send()
    for copy in kept:
        copy.wait()


def gather_call(x, w, k):
    vmem = pl.BlockSpec(memory_space=pltpu.VMEM)
    any_space = pl.BlockSpec(memory_space=pl.ANY)
    dma = pltpu.SemaphoreType.DMA
    return pl.pallas_call(
        gather_kernel,
        out_shape=[
            jax.ShapeDtypeStruct(x.shape, x.dtype),
            jax.ShapeDtypeStruct((2, 16) + w.shape, w.dtype),
            jax.ShapeDtypeStruct((2,) + k.shape, k.dtype),
        ],
        in_specs=[vmem] * 3,
        out_specs=[any_space] * 3,
        scratch_shapes=[dma((n,)) for n in (3, 3, 6, 6, 8, 8, 16, 16, 3)],
        compiler_params=pltpu.CompilerParams(collective_id=0, has_side_effects=True),
        name="gather_weights",
    )(x, w, k)


def reduce_kernel(factor, wg_ref, st_ref, out_ref, sto_ref, *scratch):
    cgot, ysend, ygot, acc, xsend, xgot, zsend, zgot, ssend, sgot = scratch[:10]
    cs, cr, ys, yr, xs, xr, zs, zr, ss, sr = scratch[10:]
    dp, sec, z, x, c = places()
    over = (dp, 1 - sec)
    mate = (z * 4 + x * 2 + 1 - c, sec)
    side_chip = (z * 4 + (1 - x) * 2 + c, sec)
    line = [((z + h) % 4 * 4 + x * 2 + c, sec) for h in (1, 2, 3)]
    greet([over, mate, side_chip] + line)
    f32 = jnp.float32
    secs = (1 - sec, sec)
    block = [(z + 1 + k) % 4 for k in range(4)]
    sends = []

    def go(src, dst, sems, slot, there):
        copy = remote(src, dst, sems, slot, there)
        copy.start()
        sends.append(copy)
        return copy

    core = {}
    for kind in range(2):
        for k in range(4):
            core[kind, k] = go(
                wg_ref.at[secs[kind], block[k], :, 1 - c],
                cgot.at[kind, k],
                (cs, cr),
                4 * kind + k,
                mate,
            )
    small = [go(st_ref.at[1 - sec], sgot.at[0], (ss, sr), 0, over)]
    small_to = [mate, side_chip, (dp + 4 - 8 * (z % 2), sec), ((dp + 8) % 16, sec)]

    def small_step(n):
        small[n].wait_recv()
        value = (st_ref[sec] if n == 0 else ssend[n - 1]) + sgot[n]
        if n == 4:
            sto_ref[...] = value * factor
        else:
            ssend[n] = value
            small.append(go(ssend.at[n], sgot.at[n + 1], (ss, sr), n + 1, small_to[n]))

    y_c = []
    for k in range(4):
        core[0, k].wait_recv()
        for h in range(2):
            ysend[k, h] = (
                wg_ref[1 - sec, block[k], h, c].astype(f32) + cgot[0, k, h].astype(f32)
            ).astype(jnp.bfloat16)
        y_c.append(go(ysend.at[k], ygot.at[k], (ys, yr), k, over))
    x_c = []
    z_c = []
    for k in range(5):
        if k < 4:
            core[1, k].wait_recv()
            y_c[k].wait_recv()

            def summed(h):
                return (
                    wg_ref[sec, block[k], h, c].astype(f32)
                    + cgot[1, k, h].astype(f32)
                    + ygot[k, h].astype(f32)
                )

            xsend[k] = summed(1 - x).astype(jnp.bfloat16)
            x_c.append(go(xsend.at[k], xgot.at[k], (xs, xr), k, side_chip))
            acc[k] = summed(x)
        if k > 0:
            x_c[k - 1].wait_recv()
            value = acc[k - 1] + xgot[k - 1].astype(f32)
            if k < 4:
                zsend[k - 1] = value.astype(jnp.bfloat16)
                z_c.append(go(zsend.at[k - 1], zgot.at[k - 1], (zs, zr), k - 1, line[k - 1]))
            else:
                acc[3] = value
        small_step(k)
    total = acc[3]
    for k in range(3):
        z_c[k].wait_recv()
        total = total + zgot[k].astype(f32)
    out_ref[...] = total * factor
    for copy in sends:
        copy.wait_send()


def reduce_call(factor, wg, st):
    _, channels, _ = wg.shape
    depth = channels // 16
    vmem = pl.BlockSpec(memory_space=pltpu.VMEM)
    dma = pltpu.SemaphoreType.DMA
    bf16, f32 = jnp.bfloat16, jnp.float32
    return pl.pallas_call(
        functools.partial(reduce_kernel, factor),
        out_shape=[
            jax.ShapeDtypeStruct((depth, channels), f32),
            jax.ShapeDtypeStruct(st.shape[1:], f32),
        ],
        in_specs=[vmem] * 2,
        out_specs=[vmem] * 2,
        scratch_shapes=[
            pltpu.VMEM((2, 4, 2, depth, channels), bf16),
            pltpu.VMEM((4, 2, depth, channels), bf16),
            pltpu.VMEM((4, 2, depth, channels), bf16),
            pltpu.VMEM((4, depth, channels), f32),
            pltpu.VMEM((4, depth, channels), bf16),
            pltpu.VMEM((4, depth, channels), bf16),
            pltpu.VMEM((3, depth, channels), bf16),
            pltpu.VMEM((3, depth, channels), bf16),
            pltpu.VMEM((4,) + st.shape[1:], f32),
            pltpu.VMEM((5,) + st.shape[1:], f32),
        ]
        + [dma((n,)) for n in (8, 8, 4, 4, 4, 4, 3, 3, 5, 5)],
        compiler_params=pltpu.CompilerParams(collective_id=1, has_side_effects=True),
        name="reduce_grads",
    )(wg.reshape(2, 4, 2, 2, depth, channels), st)


def local(
    section_inputs, cotangent, sessions, point_weight, spatial_kernel, temporal_kernel, readout
):
    mine = lax.axis_index("section")
    _, clip_count, frames, side, _, channels = section_inputs.shape
    cells = side * side
    part = clip_count // 2
    f32 = jnp.float32

    def by_cell(block):
        last = block.shape[-1]
        return block.reshape(-1, frames, cells, last).transpose(0, 2, 1, 3).reshape(-1, last)

    taps = temporal_kernel.shape[1]
    halves = by_cell(section_inputs[0]).reshape(2, -1, channels)
    cot = by_cell(lax.dynamic_slice_in_dim(cotangent, mine * part, part, 0))
    sess = lax.dynamic_slice_in_dim(sessions, mine * part, part, 0)
    spare = jnp.zeros((16 - 9 - taps, channels), f32)
    kernels = jnp.concatenate([spatial_kernel[0], temporal_kernel[0], spare], axis=0)
    x_both, w_both, k_both = gather_call(halves, point_weight[0], kernels)
    wg, st = both_call(
        frames, side, taps, sess, x_both, cot, readout, w_both.reshape(2, channels, channels), k_both
    )
    factor = 1.0 / math.sqrt(clip_count * lax.axis_size("dp") * frames * cells)
    grads, small = reduce_call(factor, wg, st)
    return (grads[None], small[:9][None], small[9 : 9 + taps][None])


def solution(mesh):
    halves = mesh.shape["section"] == 2 and mesh.shape["dp"] == 16
    return jax.shard_map(
        local if halves else pipelined,
        mesh=mesh,
        in_specs=(
            P("section", "dp", None, None, None, None),
            P("dp", None, None, None, None),
            P("dp"),
            P("section", "dp", None),
            P("section", None, None),
            P("section", None, None),
            P(),
        ),
        out_specs=(P("section", "dp", None), P("section", None, None), P("section", None, None)),
        check_vma=False,
    )
```

```python
import functools
import math

import jax
import jax.numpy as jnp
from jax import lax
from jax.experimental import pallas as pl
from jax.experimental.pallas import tpu as pltpu
from jax.sharding import PartitionSpec as P

INV_ROOT_TWO = 0.7071067811865476
INV_ROOT_TAU = 0.3989422804014327
LANES = 128
MESH = pl.DeviceIdType.MESH


def from_behind(block, axis, distance):
    devices = range(lax.axis_size(axis))
    route = [(i - distance, i) for i in devices if i - distance in devices]
    return lax.ppermute(block, axis, route)


def gelu_value(pre_act):
    return 0.5 * pre_act * (1.0 + jax.scipy.special.erf(pre_act * INV_ROOT_TWO))


def gelu_slope(pre_act):
    return (
        0.5 * (1.0 + jax.scipy.special.erf(pre_act * INV_ROOT_TWO))
        + pre_act * jnp.exp(-0.5 * pre_act * pre_act) * INV_ROOT_TAU
    )


def spatial_pad(field_in):
    pad_spec = [(0, 0)] * (field_in.ndim - 3) + [(1, 1), (1, 1), (0, 0)]
    return jnp.pad(field_in, pad_spec)


def spatial(field_in, kernel):
    height, width = (field_in.shape[-3], field_in.shape[-2])
    padded = spatial_pad(field_in)
    summed = jnp.zeros_like(field_in)
    for row_off in range(3):
        for col_off in range(3):
            summed = (
                summed
                + kernel[3 * row_off + col_off]
                * padded[..., row_off : row_off + height, col_off : col_off + width, :]
            )
    return summed


def spatial_back(grad_in, kernel):
    height, width = (grad_in.shape[-3], grad_in.shape[-2])
    padded = spatial_pad(grad_in)
    summed = jnp.zeros_like(grad_in)
    for row_off in range(3):
        for col_off in range(3):
            summed = (
                summed
                + kernel[3 * row_off + col_off]
                * padded[
                    ..., 2 - row_off : 2 - row_off + height, 2 - col_off : 2 - col_off + width, :
                ]
            )
    return summed


def spatial_kernel_grad(field_in, grad_in):
    height, width = (field_in.shape[-3], field_in.shape[-2])
    padded = spatial_pad(field_in)
    axes_all = tuple(range(field_in.ndim - 1))
    parts = []
    for row_off in range(3):
        for col_off in range(3):
            parts.append(
                jnp.sum(
                    padded[..., row_off : row_off + height, col_off : col_off + width, :] * grad_in,
                    axis=axes_all,
                )
            )
    return jnp.stack(parts)


def front_pad(field_in, tap_count):
    pad_spec = [(0, 0)] * (field_in.ndim - 4) + [(tap_count - 1, 0), (0, 0), (0, 0), (0, 0)]
    return jnp.pad(field_in, pad_spec)


def temporal(field_in, kernel):
    tap_count = kernel.shape[0]
    frames = field_in.shape[-4]
    padded = front_pad(field_in, tap_count)
    summed = jnp.zeros_like(field_in)
    for delay in range(tap_count):
        first = tap_count - 1 - delay
        summed = summed + kernel[delay] * padded[..., first : first + frames, :, :, :]
    return summed


def temporal_back(grad_in, kernel):
    tap_count = kernel.shape[0]
    frames = grad_in.shape[-4]
    pad_spec = [(0, 0)] * (grad_in.ndim - 4) + [(0, tap_count - 1), (0, 0), (0, 0), (0, 0)]
    padded = jnp.pad(grad_in, pad_spec)
    summed = jnp.zeros_like(grad_in)
    for delay in range(tap_count):
        summed = summed + kernel[delay] * padded[..., delay : delay + frames, :, :, :]
    return summed


def temporal_kernel_grad(field_in, grad_in, tap_count):
    frames = field_in.shape[-4]
    padded = front_pad(field_in, tap_count)
    axes_all = tuple(range(field_in.ndim - 1))
    parts = []
    for delay in range(tap_count):
        first = tap_count - 1 - delay
        parts.append(jnp.sum(padded[..., first : first + frames, :, :, :] * grad_in, axis=axes_all))
    return jnp.stack(parts)


def section_back(inputs, grad_out, s_kernel, t_kernel, hidden_of):
    field_in = inputs.astype(jnp.float32)
    spread = spatial(field_in, s_kernel)
    pre_act = temporal(spread, t_kernel)
    hidden = gelu_value(pre_act).astype(jnp.bfloat16)
    channels = inputs.shape[-1]
    flat_grad = grad_out.reshape(-1, channels)
    flat_hidden = hidden.reshape(-1, channels)
    hidden_grad = hidden_of(flat_grad).reshape(pre_act.shape)
    pre_grad = hidden_grad * gelu_slope(pre_act)
    spread_grad = temporal_back(pre_grad, t_kernel)
    in_grad = (grad_out.astype(jnp.float32) + spatial_back(spread_grad, s_kernel)).astype(
        jnp.bfloat16
    )
    weight_grad = jnp.dot(flat_hidden.T, flat_grad, preferred_element_type=jnp.float32)
    s_part = spatial_kernel_grad(field_in, spread_grad)
    t_part = temporal_kernel_grad(spread, pre_grad, t_kernel.shape[0])
    return (in_grad, weight_grad, s_part, t_part)


def pipelined(
    section_inputs, cotangent, sessions, point_weight, spatial_kernel, temporal_kernel, readout
):
    section_count = lax.axis_size("section")
    my_section = lax.axis_index("section")
    inputs = section_inputs[0]
    s_kernel = spatial_kernel[0]
    t_kernel = temporal_kernel[0]
    weight_shard = point_weight[0]
    clip_count = inputs.shape[0]
    channels = inputs.shape[-1]
    chosen = jnp.take(readout, sessions, axis=0)
    top_grads = jnp.einsum(
        "cfhwr,crk->cfhwk", cotangent, chosen, preferred_element_type=jnp.float32
    ).astype(jnp.bfloat16)
    block_size = 2
    step_count = clip_count // block_size
    tick_count = step_count + section_count - 1
    full_weight = lax.all_gather(weight_shard, "dp", axis=0, tiled=True)

    def hidden_of(flat_grad):
        return jnp.dot(flat_grad, full_weight.T, preferred_element_type=jnp.float32)

    block_shape = (block_size,) + inputs.shape[1:]

    def tick(tick_index, state_now):
        incoming, w_sum, s_sum, t_sum = state_now
        clip_step = tick_index - (section_count - 1 - my_section)
        is_live = (clip_step >= 0) & (clip_step < step_count)
        first_clip = jnp.clip(clip_step, 0, step_count - 1) * block_size
        inputs_block = lax.dynamic_slice_in_dim(inputs, first_clip, block_size, 0)
        top_block = lax.dynamic_slice_in_dim(top_grads, first_clip, block_size, 0)
        grad_out = jnp.where(my_section == section_count - 1, top_block, incoming)

        def live_work(sums):
            in_grad, w_part, s_part, t_part = section_back(
                inputs_block, grad_out, s_kernel, t_kernel, hidden_of
            )
            return (in_grad, sums[0] + w_part, sums[1] + s_part, sums[2] + t_part)

        def dead_work(sums):
            return (jnp.zeros(block_shape, jnp.bfloat16), sums[0], sums[1], sums[2])

        in_grad, w_new, s_new, t_new = lax.cond(
            is_live, live_work, dead_work, (w_sum, s_sum, t_sum)
        )
        passed = from_behind(in_grad, "section", -1)
        return (passed, w_new, s_new, t_new)

    start_state = (
        jnp.zeros(block_shape, jnp.bfloat16),
        jnp.zeros((channels, channels), jnp.float32),
        jnp.zeros((9, channels), jnp.float32),
        jnp.zeros(t_kernel.shape, jnp.float32),
    )
    finals = lax.fori_loop(0, tick_count, tick, start_state)
    weight_grads = lax.psum_scatter(finals[1], "dp", scatter_dimension=0, tiled=True)
    s_total, t_total = lax.psum((finals[2], finals[3]), "dp")
    rows_all = (
        clip_count * lax.axis_size("dp") * inputs.shape[1] * inputs.shape[2] * inputs.shape[3]
    )
    factor = 1.0 / math.sqrt(rows_all)
    return ((weight_grads * factor)[None], (s_total * factor)[None], (t_total * factor)[None])


def section_work(
    first, frames, side, mine, sess_ref, x_ref, g_in_ref, read_ref, w_ref, sk_ref, tk_ref, wg_ref,
    st_ref, ing_ref, g_ref, hg_ref, hid_ref, acc_ref, middle
):
    taps = tk_ref.shape[0]
    cells = side * side
    clip_rows = cells * frames
    channels = x_ref.shape[1]
    rows = x_ref.shape[0]
    clips = rows // clip_rows
    if first:
        for clip in range(clips):
            span = pl.ds(clip * clip_rows, clip_rows)
            g_ref[span, :] = jnp.dot(
                g_in_ref[mine, span, :],
                read_ref[sess_ref[mine * clips + clip]],
                preferred_element_type=jnp.float32,
            ).astype(jnp.bfloat16)
    hg_ref[...] = lax.dot_general(
        g_ref[...], w_ref[...].reshape(channels, channels), (((1,), (1,)), ((), ())), preferred_element_type=jnp.float32
    )
    acc_ref[...] = jnp.zeros_like(acc_ref)
    frame_of = lax.broadcasted_iota(jnp.int32, (frames, LANES), 0)
    chunks = channels // LANES

    def step(index, carry):
        clip = index // chunks
        lanes = pl.ds(pl.multiple_of((index % chunks) * LANES, LANES), LANES)
        span = pl.ds(pl.multiple_of(clip * clip_rows, clip_rows), clip_rows)

        def tile(value):
            return jnp.broadcast_to(value, (frames, LANES))

        s_taps = [tile(sk_ref[k, :, lanes]) for k in range(9)]
        t_taps = [tile(tk_ref[d, :, lanes]) for d in range(taps)]
        t_front = [jnp.where(frame_of >= d, t_taps[d], 0.0) for d in range(taps)]
        t_tail = [jnp.where(frame_of < frames - d, t_taps[d], 0.0) for d in range(taps)]
        x_all = x_ref[span, lanes].astype(jnp.float32)
        hg_all = hg_ref[span, lanes]
        x = [x_all[c * frames : (c + 1) * frames] for c in range(cells)]
        inside = lambda i, j: 0 <= i < side and 0 <= j < side
        spread, sgrad, hidden = [], [], []
        t_sums = [None] * taps
        for i in range(side):
            for j in range(side):
                total = None
                for r in range(3):
                    for q in range(3):
                        if inside(i + r - 1, j + q - 1):
                            term = s_taps[3 * r + q] * x[(i + r - 1) * side + j + q - 1]
                            total = term if total is None else total + term
                pre = t_taps[0] * total
                for d in range(1, taps):
                    pre = pre + t_front[d] * pltpu.roll(total, d, 0)
                half = 0.5 + 0.5 * lax.erf(pre * INV_ROOT_TWO)
                hidden.append(pre * half)
                slope = half + pre * jnp.exp(-0.5 * pre * pre) * INV_ROOT_TAU
                c = i * side + j
                pgrad = hg_all[c * frames : (c + 1) * frames] * slope
                back = t_taps[0] * pgrad
                for d in range(taps):
                    moved = pgrad if d == 0 else pltpu.roll(pgrad, frames - d, 0)
                    if d:
                        back = back + t_tail[d] * moved
                    part = total * moved
                    t_sums[d] = part if t_sums[d] is None else t_sums[d] + part
                sgrad.append(back)
        hid_ref[span, lanes] = jnp.concatenate(hidden, axis=0).astype(jnp.bfloat16)
        for d in range(taps):
            acc_ref[9 + d, :, lanes] += t_sums[d]
        s_sums = [None] * 9
        for i in range(side):
            for j in range(side):
                for r in range(3):
                    for q in range(3):
                        if inside(i + r - 1, j + q - 1):
                            part = x[(i + r - 1) * side + j + q - 1] * sgrad[i * side + j]
                            k = 3 * r + q
                            s_sums[k] = part if s_sums[k] is None else s_sums[k] + part
        for k in range(9):
            acc_ref[k, :, lanes] += s_sums[k]
        if first:
            out = []
            for i in range(side):
                for j in range(side):
                    total = None
                    for r in range(3):
                        for q in range(3):
                            if inside(i - r + 1, j - q + 1):
                                term = s_taps[3 * r + q] * sgrad[(i - r + 1) * side + j - q + 1]
                                total = term if total is None else total + term
                    out.append(total)
            ing_ref[span, lanes] = (
                g_ref[span, lanes].astype(jnp.float32) + jnp.concatenate(out, axis=0)
            ).astype(jnp.bfloat16)
        return carry

    if middle is None:
        lax.fori_loop(0, clips * chunks, step, 0)
    else:
        lax.fori_loop(0, clips * chunks // 2, step, 0)
        middle()
        lax.fori_loop(clips * chunks // 2, clips * chunks, step, 0)
    wg = lax.dot_general(
        hid_ref[...], g_ref[...], (((0,), (0,)), ((), ())), preferred_element_type=jnp.float32
    )
    wg_ref[...] = wg.astype(wg_ref.dtype).reshape(wg_ref.shape)
    wide = lax.broadcasted_iota(jnp.int32, (frames, channels), 0)
    st_ref[...] = jnp.zeros_like(st_ref)
    for k in range(9):
        st_ref[k : k + 1, :] = jnp.sum(acc_ref[k], axis=0, keepdims=True)
    for d in range(taps):
        kept = jnp.where(wide < frames - d, acc_ref[9 + d], 0.0)
        st_ref[9 + d : 10 + d, :] = jnp.sum(kept, axis=0, keepdims=True)


def places():
    dp = lax.axis_index("dp")
    sec = lax.axis_index("section")
    return dp, sec, dp // 4, (dp // 2) % 2, dp % 2


def greet(partners):
    barrier = pltpu.get_barrier_semaphore()
    for there in partners:
        pl.semaphore_signal(barrier, inc=1, device_id=there, device_id_type=MESH)
    pl.semaphore_wait(barrier, len(partners))


def remote(src, dst, sems, slot, there):
    return pltpu.make_async_remote_copy(
        src_ref=src,
        dst_ref=dst,
        send_sem=sems[0].at[slot],
        recv_sem=sems[1].at[slot],
        device_id=there,
        device_id_type=MESH,
    )


def whole_kernel(
    frames,
    side,
    factor,
    sess_ref,
    x_ref,
    cot_ref,
    read_ref,
    w_ref,
    sk_ref,
    tk_ref,
    out_ref,
    so_ref,
    to_ref,
    *scratch,
):
    xo_ref, wo_ref, sko_ref, tko_ref, wg_ref, st_ref = scratch[:6]
    work = scratch[6:11]
    cgot, xsend, xgot, acc, ysend, ygot, zsend, zgot, ssend, sgot = scratch[11:21]
    ays, ayr, azs, azr, axs, axr, acs, acr, own_sem = scratch[21:30]
    cs, cr, xs, xr, ys, yr, zs, zr, ss, sr = scratch[30:]
    f32, bf16 = jnp.float32, jnp.bfloat16
    taps = tk_ref.shape[0]
    channels = w_ref.shape[1]
    dp, sec, z, x, c = places()
    over = (dp, 1 - sec)
    mate = (z * 4 + x * 2 + 1 - c, sec)
    side_chip = (z * 4 + (1 - x) * 2 + c, sec)
    line = [((z + h) % 4 * 4 + x * 2 + c, sec) for h in (1, 2, 3)]
    greet([over, mate, side_chip] + line)
    secs = (sec, 1 - sec)
    block = [(z + 1 + k) % 4 for k in range(4)]
    sends = []

    def go(src, dst, sems, slot, there):
        copy = remote(src, dst, sems, slot, there)
        copy.start()
        sends.append(copy)
        return copy

    slot_of = wo_ref.at[sec, dp]
    y_w = go(w_ref, slot_of, (ays, ayr), 0, over)
    z_w = {}
    x_w = {}
    c_w = {}
    for h in range(3):
        z_w[0, h] = go(w_ref, slot_of, (azs, azr), h, line[h])
    x_w[0, 0] = go(w_ref, slot_of, (axs, axr), 0, side_chip)
    c_w[0, 0] = go(w_ref, slot_of, (acs, acr), 0, mate)
    y_rest = [
        go(sk_ref, sko_ref.at[sec], (ays, ayr), 1, over),
        go(tk_ref, tko_ref.at[sec], (ays, ayr), 2, over),
        go(x_ref.at[1 - sec], xo_ref.at[sec], (ays, ayr), 3, over),
    ]
    kept = [
        pltpu.make_async_copy(w_ref, slot_of, own_sem.at[0]),
        pltpu.make_async_copy(sk_ref, sko_ref.at[sec], own_sem.at[1]),
        pltpu.make_async_copy(tk_ref, tko_ref.at[sec], own_sem.at[2]),
        pltpu.make_async_copy(x_ref.at[sec], xo_ref.at[sec], own_sem.at[3]),
    ]
    for copy in kept:
        copy.start()
    y_w.wait_recv()
    held = wo_ref.at[1 - sec, dp]
    for h in range(3):
        z_w[1, h] = go(held, held, (azs, azr), 3 + h, line[h])
    x_w[1, 0] = go(held, held, (axs, axr), 4, side_chip)
    c_w[1, 0] = go(held, held, (acs, acr), 8, mate)
    for h in range(3):
        source = (z + 3 - h) % 4 * 4 + x * 2 + c
        for kind in range(2):
            z_w[kind, h].wait_recv()
            held = wo_ref.at[secs[kind], source]
            x_w[kind, h + 1] = go(held, held, (axs, axr), 4 * kind + h + 1, side_chip)
            c_w[kind, h + 1] = go(held, held, (acs, acr), 8 * kind + h + 1, mate)
    for h in range(4):
        source = (z + 4 - h) % 4 * 4 + (1 - x) * 2 + c
        for kind in range(2):
            x_w[kind, h].wait_recv()
            held = wo_ref.at[secs[kind], source]
            c_w[kind, h + 4] = go(held, held, (acs, acr), 8 * kind + h + 4, mate)
    for copy in c_w.values():
        copy.wait_recv()
    for copy in y_rest:
        copy.wait_recv()
    for copy in kept:
        copy.wait()

    def compute(s, middle):
        ing_ref, g_ref, hg_ref, hid_ref, acc_ref = work
        section_work(
            s == 1,
            frames,
            side,
            sec,
            sess_ref,
            xo_ref.at[s],
            cot_ref,
            read_ref,
            wo_ref.at[s],
            sko_ref.at[s],
            tko_ref.at[s],
            wg_ref.at[s],
            st_ref.at[s],
            ing_ref,
            g_ref if s == 1 else ing_ref,
            hg_ref,
            hid_ref,
            acc_ref,
            middle,
        )

    core = {}

    def core_stage(s):
        for k in range(4):
            core[s, k] = go(
                wg_ref.at[s, block[k], :, 1 - c], cgot.at[s, k], (cs, cr), 4 * s + k, mate
            )

    def x_stage(s):
        for k in range(4):
            core[s, k].wait_recv()
            xsend[s, k] = (
                wg_ref[s, block[k], 1 - x, c].astype(f32) + cgot[s, k, 1 - x].astype(f32)
            ).astype(bf16)
            go(xsend.at[s, k], xgot.at[s, k], (xs, xr), 4 * s + k, side_chip)

    compute(1, None)
    core_stage(1)
    compute(0, lambda: x_stage(1))
    core_stage(0)
    small = [go(st_ref.at[1 - sec], sgot.at[0], (ss, sr), 0, over)]
    small_to = [mate, side_chip, (dp + 4 - 8 * (z % 2), sec), ((dp + 8) % 16, sec)]

    def small_step(n):
        small[n].wait_recv()
        value = (st_ref[sec] if n == 0 else ssend[n - 1]) + sgot[n]
        if n == 4:
            value = value * factor
            for k in range(9):
                so_ref[k] = value[k : k + 1]
            for d in range(taps):
                to_ref[d] = value[9 + d : 10 + d]
        else:
            ssend[n] = value
            small.append(go(ssend.at[n], sgot.at[n + 1], (ss, sr), n + 1, small_to[n]))

    x_stage(0)

    def chip_pair_sum(s, k):
        remote(xsend.at[s, k], xgot.at[s, k], (xs, xr), 4 * s + k, side_chip).wait_recv()
        return (
            wg_ref[s, block[k], x, c].astype(f32)
            + cgot[s, k, x].astype(f32)
            + xgot[s, k].astype(f32)
        )

    y_c = []
    for k in range(4):
        ysend[k] = chip_pair_sum(1 - sec, k).astype(bf16)
        y_c.append(go(ysend.at[k], ygot.at[k], (ys, yr), k, over))
        if k % 2:
            small_step(k // 2)
    z_c = []
    for k in range(4):
        value = chip_pair_sum(sec, k)
        y_c[k].wait_recv()
        value = value + ygot[k].astype(f32)
        if k < 3:
            zsend[k] = value.astype(bf16)
            z_c.append(go(zsend.at[k], zgot.at[k], (zs, zr), k, line[k]))
        else:
            acc[...] = value
        if k < 3:
            small_step(2 + k)
    total = acc[...]
    for k in range(3):
        z_c[k].wait_recv()
        total = total + zgot[k].astype(f32)
    out_ref[...] = total * factor
    for copy in sends:
        copy.wait_send()


def whole_call(frames, side, factor, sess, x, cot, read, w, sk, tk):
    _, rows, channels = x.shape
    depth = w.shape[0]
    taps = tk.shape[0]
    vmem = pl.BlockSpec(memory_space=pltpu.VMEM)
    dma = pltpu.SemaphoreType.DMA
    bf16, f32 = jnp.bfloat16, jnp.float32
    wide = (depth, channels)
    return pl.pallas_call(
        functools.partial(whole_kernel, frames, side, factor),
        out_shape=[
            jax.ShapeDtypeStruct(wide, f32),
            jax.ShapeDtypeStruct(sk.shape, f32),
            jax.ShapeDtypeStruct(tk.shape, f32),
        ],
        in_specs=[pl.BlockSpec(memory_space=pltpu.SMEM)] + [vmem] * 6,
        out_specs=[vmem] * 3,
        scratch_shapes=[
            pltpu.VMEM(x.shape, bf16),
            pltpu.VMEM((2, 16) + wide, bf16),
            pltpu.VMEM((2,) + sk.shape, f32),
            pltpu.VMEM((2,) + tk.shape, f32),
            pltpu.VMEM((2, 4, 2, 2) + wide, bf16),
            pltpu.VMEM((2, 16, channels), f32),
            pltpu.VMEM((rows, channels), bf16),
            pltpu.VMEM((rows, channels), bf16),
            pltpu.VMEM((rows, channels), f32),
            pltpu.VMEM((rows, channels), bf16),
            pltpu.VMEM((9 + taps, frames, channels), f32),
            pltpu.VMEM((2, 4, 2) + wide, bf16),
            pltpu.VMEM((2, 4) + wide, bf16),
            pltpu.VMEM((2, 4) + wide, bf16),
            pltpu.VMEM(wide, f32),
            pltpu.VMEM((4,) + wide, bf16),
            pltpu.VMEM((4,) + wide, bf16),
            pltpu.VMEM((3,) + wide, bf16),
            pltpu.VMEM((3,) + wide, bf16),
            pltpu.VMEM((4, 16, channels), f32),
            pltpu.VMEM((5, 16, channels), f32),
        ]
        + [dma((n,)) for n in (4, 4, 6, 6, 8, 8, 16, 16, 4)]
        + [dma((n,)) for n in (8, 8, 8, 8, 4, 4, 3, 3, 5, 5)],
        compiler_params=pltpu.CompilerParams(
            collective_id=0, has_side_effects=True, vmem_limit_bytes=48 << 20
        ),
        name="whole_backward",
    )(sess, x, cot, read, w, sk, tk)


def local(
    section_inputs, cotangent, sessions, point_weight, spatial_kernel, temporal_kernel, readout
):
    _, clip_count, frames, side, _, channels = section_inputs.shape
    cells = side * side

    def by_cell(block):
        last = block.shape[-1]
        return block.reshape(-1, frames, cells, last).transpose(0, 2, 1, 3).reshape(-1, last)

    halves = by_cell(section_inputs[0]).reshape(2, -1, channels)
    cot = by_cell(cotangent).reshape(2, -1, cotangent.shape[-1])
    factor = 1.0 / math.sqrt(clip_count * lax.axis_size("dp") * frames * cells)
    grads, s_out, t_out = whole_call(
        frames,
        side,
        factor,
        sessions,
        halves,
        cot,
        readout,
        point_weight[0],
        spatial_kernel.transpose(1, 0, 2),
        temporal_kernel.transpose(1, 0, 2),
    )
    return (grads[None], s_out.transpose(1, 0, 2), t_out.transpose(1, 0, 2))


def solution(mesh):
    halves = mesh.shape["section"] == 2 and mesh.shape["dp"] == 16
    return jax.shard_map(
        local if halves else pipelined,
        mesh=mesh,
        in_specs=(
            P("section", "dp", None, None, None, None),
            P("dp", None, None, None, None),
            P("dp"),
            P("section", "dp", None),
            P("section", None, None),
            P("section", None, None),
            P(),
        ),
        out_specs=(P("section", "dp", None), P("section", None, None), P("section", None, None)),
        check_vma=False,
    )
```

```python
import functools
import math

import jax
import jax.numpy as jnp
from jax import lax
from jax.experimental import pallas as pl
from jax.experimental.pallas import tpu as pltpu
from jax.sharding import PartitionSpec as P

INV_ROOT_TWO = 0.7071067811865476
INV_ROOT_TAU = 0.3989422804014327
LANES = 128
MESH = pl.DeviceIdType.MESH


def from_behind(block, axis, distance):
    devices = range(lax.axis_size(axis))
    route = [(i - distance, i) for i in devices if i - distance in devices]
    return lax.ppermute(block, axis, route)


def gelu_value(pre_act):
    return 0.5 * pre_act * (1.0 + jax.scipy.special.erf(pre_act * INV_ROOT_TWO))


def gelu_slope(pre_act):
    return (
        0.5 * (1.0 + jax.scipy.special.erf(pre_act * INV_ROOT_TWO))
        + pre_act * jnp.exp(-0.5 * pre_act * pre_act) * INV_ROOT_TAU
    )


def spatial_pad(field_in):
    pad_spec = [(0, 0)] * (field_in.ndim - 3) + [(1, 1), (1, 1), (0, 0)]
    return jnp.pad(field_in, pad_spec)


def spatial(field_in, kernel):
    height, width = (field_in.shape[-3], field_in.shape[-2])
    padded = spatial_pad(field_in)
    summed = jnp.zeros_like(field_in)
    for row_off in range(3):
        for col_off in range(3):
            summed = (
                summed
                + kernel[3 * row_off + col_off]
                * padded[..., row_off : row_off + height, col_off : col_off + width, :]
            )
    return summed


def spatial_back(grad_in, kernel):
    height, width = (grad_in.shape[-3], grad_in.shape[-2])
    padded = spatial_pad(grad_in)
    summed = jnp.zeros_like(grad_in)
    for row_off in range(3):
        for col_off in range(3):
            summed = (
                summed
                + kernel[3 * row_off + col_off]
                * padded[
                    ..., 2 - row_off : 2 - row_off + height, 2 - col_off : 2 - col_off + width, :
                ]
            )
    return summed


def spatial_kernel_grad(field_in, grad_in):
    height, width = (field_in.shape[-3], field_in.shape[-2])
    padded = spatial_pad(field_in)
    axes_all = tuple(range(field_in.ndim - 1))
    parts = []
    for row_off in range(3):
        for col_off in range(3):
            parts.append(
                jnp.sum(
                    padded[..., row_off : row_off + height, col_off : col_off + width, :] * grad_in,
                    axis=axes_all,
                )
            )
    return jnp.stack(parts)


def front_pad(field_in, tap_count):
    pad_spec = [(0, 0)] * (field_in.ndim - 4) + [(tap_count - 1, 0), (0, 0), (0, 0), (0, 0)]
    return jnp.pad(field_in, pad_spec)


def temporal(field_in, kernel):
    tap_count = kernel.shape[0]
    frames = field_in.shape[-4]
    padded = front_pad(field_in, tap_count)
    summed = jnp.zeros_like(field_in)
    for delay in range(tap_count):
        first = tap_count - 1 - delay
        summed = summed + kernel[delay] * padded[..., first : first + frames, :, :, :]
    return summed


def temporal_back(grad_in, kernel):
    tap_count = kernel.shape[0]
    frames = grad_in.shape[-4]
    pad_spec = [(0, 0)] * (grad_in.ndim - 4) + [(0, tap_count - 1), (0, 0), (0, 0), (0, 0)]
    padded = jnp.pad(grad_in, pad_spec)
    summed = jnp.zeros_like(grad_in)
    for delay in range(tap_count):
        summed = summed + kernel[delay] * padded[..., delay : delay + frames, :, :, :]
    return summed


def temporal_kernel_grad(field_in, grad_in, tap_count):
    frames = field_in.shape[-4]
    padded = front_pad(field_in, tap_count)
    axes_all = tuple(range(field_in.ndim - 1))
    parts = []
    for delay in range(tap_count):
        first = tap_count - 1 - delay
        parts.append(jnp.sum(padded[..., first : first + frames, :, :, :] * grad_in, axis=axes_all))
    return jnp.stack(parts)


def section_back(inputs, grad_out, s_kernel, t_kernel, hidden_of):
    field_in = inputs.astype(jnp.float32)
    spread = spatial(field_in, s_kernel)
    pre_act = temporal(spread, t_kernel)
    hidden = gelu_value(pre_act).astype(jnp.bfloat16)
    channels = inputs.shape[-1]
    flat_grad = grad_out.reshape(-1, channels)
    flat_hidden = hidden.reshape(-1, channels)
    hidden_grad = hidden_of(flat_grad).reshape(pre_act.shape)
    pre_grad = hidden_grad * gelu_slope(pre_act)
    spread_grad = temporal_back(pre_grad, t_kernel)
    in_grad = (grad_out.astype(jnp.float32) + spatial_back(spread_grad, s_kernel)).astype(
        jnp.bfloat16
    )
    weight_grad = jnp.dot(flat_hidden.T, flat_grad, preferred_element_type=jnp.float32)
    s_part = spatial_kernel_grad(field_in, spread_grad)
    t_part = temporal_kernel_grad(spread, pre_grad, t_kernel.shape[0])
    return (in_grad, weight_grad, s_part, t_part)


def pipelined(
    section_inputs, cotangent, sessions, point_weight, spatial_kernel, temporal_kernel, readout
):
    section_count = lax.axis_size("section")
    my_section = lax.axis_index("section")
    inputs = section_inputs[0]
    s_kernel = spatial_kernel[0]
    t_kernel = temporal_kernel[0]
    weight_shard = point_weight[0]
    clip_count = inputs.shape[0]
    channels = inputs.shape[-1]
    chosen = jnp.take(readout, sessions, axis=0)
    top_grads = jnp.einsum(
        "cfhwr,crk->cfhwk", cotangent, chosen, preferred_element_type=jnp.float32
    ).astype(jnp.bfloat16)
    block_size = 2
    step_count = clip_count // block_size
    tick_count = step_count + section_count - 1
    full_weight = lax.all_gather(weight_shard, "dp", axis=0, tiled=True)

    def hidden_of(flat_grad):
        return jnp.dot(flat_grad, full_weight.T, preferred_element_type=jnp.float32)

    block_shape = (block_size,) + inputs.shape[1:]

    def tick(tick_index, state_now):
        incoming, w_sum, s_sum, t_sum = state_now
        clip_step = tick_index - (section_count - 1 - my_section)
        is_live = (clip_step >= 0) & (clip_step < step_count)
        first_clip = jnp.clip(clip_step, 0, step_count - 1) * block_size
        inputs_block = lax.dynamic_slice_in_dim(inputs, first_clip, block_size, 0)
        top_block = lax.dynamic_slice_in_dim(top_grads, first_clip, block_size, 0)
        grad_out = jnp.where(my_section == section_count - 1, top_block, incoming)

        def live_work(sums):
            in_grad, w_part, s_part, t_part = section_back(
                inputs_block, grad_out, s_kernel, t_kernel, hidden_of
            )
            return (in_grad, sums[0] + w_part, sums[1] + s_part, sums[2] + t_part)

        def dead_work(sums):
            return (jnp.zeros(block_shape, jnp.bfloat16), sums[0], sums[1], sums[2])

        in_grad, w_new, s_new, t_new = lax.cond(
            is_live, live_work, dead_work, (w_sum, s_sum, t_sum)
        )
        passed = from_behind(in_grad, "section", -1)
        return (passed, w_new, s_new, t_new)

    start_state = (
        jnp.zeros(block_shape, jnp.bfloat16),
        jnp.zeros((channels, channels), jnp.float32),
        jnp.zeros((9, channels), jnp.float32),
        jnp.zeros(t_kernel.shape, jnp.float32),
    )
    finals = lax.fori_loop(0, tick_count, tick, start_state)
    weight_grads = lax.psum_scatter(finals[1], "dp", scatter_dimension=0, tiled=True)
    s_total, t_total = lax.psum((finals[2], finals[3]), "dp")
    rows_all = (
        clip_count * lax.axis_size("dp") * inputs.shape[1] * inputs.shape[2] * inputs.shape[3]
    )
    factor = 1.0 / math.sqrt(rows_all)
    return ((weight_grads * factor)[None], (s_total * factor)[None], (t_total * factor)[None])


def section_work(
    first, frames, side, mine, sess_ref, x_ref, g_in_ref, read_ref, w_ref, sk_ref, tk_ref, wg_ref,
    st_ref, ing_ref, g_ref, hg_ref, hid_ref, acc_ref, middle, arrive
):
    taps = tk_ref.shape[0]
    cells = side * side
    clip_rows = cells * frames
    channels = x_ref.shape[1]
    rows = x_ref.shape[0]
    clips = rows // clip_rows
    if first:
        for clip in range(clips):
            span = pl.ds(clip * clip_rows, clip_rows)
            g_ref[span, :] = jnp.dot(
                g_in_ref[mine, span, :],
                read_ref[sess_ref[mine * clips + clip]],
                preferred_element_type=jnp.float32,
            ).astype(jnp.bfloat16)
    hg_ref[...] = lax.dot_general(
        g_ref[...], w_ref[...].reshape(channels, channels), (((1,), (1,)), ((), ())), preferred_element_type=jnp.float32
    )
    acc_ref[...] = jnp.zeros_like(acc_ref)
    frame_of = lax.broadcasted_iota(jnp.int32, (frames, LANES), 0)
    chunks = channels // LANES

    def step(index, carry):
        clip = index // chunks
        lanes = pl.ds(pl.multiple_of((index % chunks) * LANES, LANES), LANES)
        span = pl.ds(pl.multiple_of(clip * clip_rows, clip_rows), clip_rows)

        def tile(value):
            return jnp.broadcast_to(value, (frames, LANES))

        s_taps = [tile(sk_ref[k, :, lanes]) for k in range(9)]
        t_taps = [tile(tk_ref[d, :, lanes]) for d in range(taps)]
        t_front = [jnp.where(frame_of >= d, t_taps[d], 0.0) for d in range(taps)]
        t_tail = [jnp.where(frame_of < frames - d, t_taps[d], 0.0) for d in range(taps)]
        x_all = x_ref[span, lanes].astype(jnp.float32)
        hg_all = hg_ref[span, lanes]
        x = [x_all[c * frames : (c + 1) * frames] for c in range(cells)]
        inside = lambda i, j: 0 <= i < side and 0 <= j < side
        spread, sgrad, hidden = [], [], []
        t_sums = [None] * taps
        for i in range(side):
            for j in range(side):
                total = None
                for r in range(3):
                    for q in range(3):
                        if inside(i + r - 1, j + q - 1):
                            term = s_taps[3 * r + q] * x[(i + r - 1) * side + j + q - 1]
                            total = term if total is None else total + term
                pre = t_taps[0] * total
                for d in range(1, taps):
                    pre = pre + t_front[d] * pltpu.roll(total, d, 0)
                half = 0.5 + 0.5 * lax.erf(pre * INV_ROOT_TWO)
                hidden.append(pre * half)
                slope = half + pre * jnp.exp(-0.5 * pre * pre) * INV_ROOT_TAU
                c = i * side + j
                pgrad = hg_all[c * frames : (c + 1) * frames] * slope
                back = t_taps[0] * pgrad
                for d in range(taps):
                    moved = pgrad if d == 0 else pltpu.roll(pgrad, frames - d, 0)
                    if d:
                        back = back + t_tail[d] * moved
                    part = total * moved
                    t_sums[d] = part if t_sums[d] is None else t_sums[d] + part
                sgrad.append(back)
        hid_ref[span, lanes] = jnp.concatenate(hidden, axis=0).astype(jnp.bfloat16)
        for d in range(taps):
            acc_ref[9 + d, :, lanes] += t_sums[d]
        s_sums = [None] * 9
        for i in range(side):
            for j in range(side):
                for r in range(3):
                    for q in range(3):
                        if inside(i + r - 1, j + q - 1):
                            part = x[(i + r - 1) * side + j + q - 1] * sgrad[i * side + j]
                            k = 3 * r + q
                            s_sums[k] = part if s_sums[k] is None else s_sums[k] + part
        for k in range(9):
            acc_ref[k, :, lanes] += s_sums[k]
        if first:
            out = []
            for i in range(side):
                for j in range(side):
                    total = None
                    for r in range(3):
                        for q in range(3):
                            if inside(i - r + 1, j - q + 1):
                                term = s_taps[3 * r + q] * sgrad[(i - r + 1) * side + j - q + 1]
                                total = term if total is None else total + term
                    out.append(total)
            ing_ref[span, lanes] = (
                g_ref[span, lanes].astype(jnp.float32) + jnp.concatenate(out, axis=0)
            ).astype(jnp.bfloat16)
        return carry


    def clip_step(clip, carry):
        arrive(clip)
        return lax.fori_loop(
            0, chunks, lambda index, kept: step(clip * chunks + index, kept), carry
        )

    lax.fori_loop(0, clips // 2, clip_step, 0)
    middle()
    lax.fori_loop(clips // 2, clips, clip_step, 0)
    wg = lax.dot_general(
        hid_ref[...], g_ref[...], (((0,), (0,)), ((), ())), preferred_element_type=jnp.float32
    )
    wg_ref[...] = wg.astype(wg_ref.dtype).reshape(wg_ref.shape)
    wide = lax.broadcasted_iota(jnp.int32, (frames, channels), 0)
    st_ref[...] = jnp.zeros_like(st_ref)
    for k in range(9):
        st_ref[k : k + 1, :] = jnp.sum(acc_ref[k], axis=0, keepdims=True)
    for d in range(taps):
        kept = jnp.where(wide < frames - d, acc_ref[9 + d], 0.0)
        st_ref[9 + d : 10 + d, :] = jnp.sum(kept, axis=0, keepdims=True)


def places():
    dp = lax.axis_index("dp")
    sec = lax.axis_index("section")
    return dp, sec, dp // 4, (dp // 2) % 2, dp % 2


def greet(partners):
    barrier = pltpu.get_barrier_semaphore()
    for there in partners:
        pl.semaphore_signal(barrier, inc=1, device_id=there, device_id_type=MESH)
    pl.semaphore_wait(barrier, len(partners))


def remote(src, dst, sems, slot, there):
    return pltpu.make_async_remote_copy(
        src_ref=src,
        dst_ref=dst,
        send_sem=sems[0].at[slot],
        recv_sem=sems[1].at[slot],
        device_id=there,
        device_id_type=MESH,
    )


def whole_kernel(
    frames,
    side,
    factor,
    sess_ref,
    x_ref,
    cot_ref,
    read_ref,
    w_ref,
    sk_ref,
    tk_ref,
    out_ref,
    so_ref,
    to_ref,
    *scratch,
):
    xo_ref, wo_ref, sko_ref, tko_ref, wg_ref, st_ref = scratch[:6]
    work = scratch[6:11]
    cgot, xsend, xgot, acc, ysend, ygot, zsend, zgot, ssend, sgot = scratch[11:21]
    ays, ayr, azs, azr, axs, axr, acs, acr, own_sem = scratch[21:30]
    cs, cr, xs, xr, ys, yr, zs, zr, ss, sr = scratch[30:]
    f32, bf16 = jnp.float32, jnp.bfloat16
    taps = tk_ref.shape[0]
    channels = w_ref.shape[1]
    dp, sec, z, x, c = places()
    over = (dp, 1 - sec)
    mate = (z * 4 + x * 2 + 1 - c, sec)
    side_chip = (z * 4 + (1 - x) * 2 + c, sec)
    line = [((z + h) % 4 * 4 + x * 2 + c, sec) for h in (1, 2, 3)]
    greet([over, mate, side_chip] + line)
    secs = (sec, 1 - sec)
    block = [(z + 1 + k) % 4 for k in range(4)]
    sends = []

    def go(src, dst, sems, slot, there):
        copy = remote(src, dst, sems, slot, there)
        copy.start()
        sends.append(copy)
        return copy

    slot_of = wo_ref.at[sec, dp]
    y_w = go(w_ref, slot_of, (ays, ayr), 0, over)
    z_w = {}
    x_w = {}
    c_w = {}
    for h in range(3):
        z_w[0, h] = go(w_ref, slot_of, (azs, azr), h, line[h])
    x_w[0, 0] = go(w_ref, slot_of, (axs, axr), 0, side_chip)
    c_w[0, 0] = go(w_ref, slot_of, (acs, acr), 0, mate)
    y_rest = [
        go(sk_ref, sko_ref.at[sec], (ays, ayr), 1, over),
        go(tk_ref, tko_ref.at[sec], (ays, ayr), 2, over),
    ]
    clip_rows = side * side * frames
    clips = x_ref.shape[1] // clip_rows

    def clip_copy(clip):
        span = pl.ds(pl.multiple_of(clip * clip_rows, clip_rows), clip_rows)
        return remote(
            x_ref.at[1 - sec, span], xo_ref.at[sec, span], (ays, ayr), 3 + clip, over
        )

    for clip in range(clips):
        copy = clip_copy(clip)
        copy.start()
        sends.append(copy)
    kept = [
        pltpu.make_async_copy(w_ref, slot_of, own_sem.at[0]),
        pltpu.make_async_copy(sk_ref, sko_ref.at[sec], own_sem.at[1]),
        pltpu.make_async_copy(tk_ref, tko_ref.at[sec], own_sem.at[2]),
        pltpu.make_async_copy(x_ref.at[sec], xo_ref.at[sec], own_sem.at[3]),
    ]
    for copy in kept:
        copy.start()
    y_w.wait_recv()
    held = wo_ref.at[1 - sec, dp]
    for h in range(3):
        z_w[1, h] = go(held, held, (azs, azr), 3 + h, line[h])
    x_w[1, 0] = go(held, held, (axs, axr), 4, side_chip)
    c_w[1, 0] = go(held, held, (acs, acr), 8, mate)

    def slot_copy(s, source, sems, base, h, there):
        kind = (s + sec) % 2
        held = wo_ref.at[s, source]
        return remote(held, held, sems, base * kind + h, there)

    def pass_on(copy):
        copy.start()
        sends.append(copy)

    def from_line(s, h):
        source = (z + 3 - h) % 4 * 4 + x * 2 + c
        slot_copy(s, source, (azs, azr), 3, h, line[h]).wait_recv()
        pass_on(slot_copy(s, source, (axs, axr), 4, h + 1, side_chip))
        pass_on(slot_copy(s, source, (acs, acr), 8, h + 1, mate))

    def from_side(s):
        for h in range(4):
            source = (z + 4 - h) % 4 * 4 + (1 - x) * 2 + c
            slot_copy(s, source, (axs, axr), 4, h, side_chip).wait_recv()
            pass_on(slot_copy(s, source, (acs, acr), 8, h + 4, mate))

    def from_mate(s):
        for h in range(8):
            slot_copy(s, dp, (acs, acr), 8, h, mate).wait_recv()

    for h in range(3):
        from_line(1, h)
        from_line(0, h)
    from_side(1)
    from_mate(1)
    for copy in y_rest:
        copy.wait_recv()
    for copy in kept:
        copy.wait()

    def compute(s, middle):
        def arrive(clip):
            @pl.when(sec != s)
            def _():
                clip_copy(clip).wait_recv()

        ing_ref, g_ref, hg_ref, hid_ref, acc_ref = work
        section_work(
            s == 1,
            frames,
            side,
            sec,
            sess_ref,
            xo_ref.at[s],
            cot_ref,
            read_ref,
            wo_ref.at[s],
            sko_ref.at[s],
            tko_ref.at[s],
            wg_ref.at[s],
            st_ref.at[s],
            ing_ref,
            g_ref if s == 1 else ing_ref,
            hg_ref,
            hid_ref,
            acc_ref,
            middle,
            arrive,
        )

    core = {}

    def core_stage(s):
        for k in range(4):
            core[s, k] = go(
                wg_ref.at[s, block[k], :, 1 - c], cgot.at[s, k], (cs, cr), 4 * s + k, mate
            )

    def x_stage(s):
        for k in range(4):
            core[s, k].wait_recv()
            xsend[s, k] = (
                wg_ref[s, block[k], 1 - x, c].astype(f32) + cgot[s, k, 1 - x].astype(f32)
            ).astype(bf16)
            go(xsend.at[s, k], xgot.at[s, k], (xs, xr), 4 * s + k, side_chip)

    compute(1, lambda: from_side(0))
    core_stage(1)
    from_mate(0)
    compute(0, lambda: x_stage(1))
    core_stage(0)
    small = [go(st_ref.at[1 - sec], sgot.at[0], (ss, sr), 0, over)]
    small_to = [mate, side_chip, (dp + 4 - 8 * (z % 2), sec), ((dp + 8) % 16, sec)]

    def small_step(n):
        small[n].wait_recv()
        value = (st_ref[sec] if n == 0 else ssend[n - 1]) + sgot[n]
        if n == 4:
            value = value * factor
            for k in range(9):
                so_ref[k] = value[k : k + 1]
            for d in range(taps):
                to_ref[d] = value[9 + d : 10 + d]
        else:
            ssend[n] = value
            small.append(go(ssend.at[n], sgot.at[n + 1], (ss, sr), n + 1, small_to[n]))

    x_stage(0)

    def chip_pair_sum(s, k):
        remote(xsend.at[s, k], xgot.at[s, k], (xs, xr), 4 * s + k, side_chip).wait_recv()
        return (
            wg_ref[s, block[k], x, c].astype(f32)
            + cgot[s, k, x].astype(f32)
            + xgot[s, k].astype(f32)
        )

    y_c = []
    for k in range(4):
        ysend[k] = chip_pair_sum(1 - sec, k).astype(bf16)
        y_c.append(go(ysend.at[k], ygot.at[k], (ys, yr), k, over))
        if k % 2:
            small_step(k // 2)
    z_c = []
    for k in range(4):
        value = chip_pair_sum(sec, k)
        y_c[k].wait_recv()
        value = value + ygot[k].astype(f32)
        if k < 3:
            zsend[k] = value.astype(bf16)
            z_c.append(go(zsend.at[k], zgot.at[k], (zs, zr), k, line[k]))
        else:
            acc[...] = value
        if k < 3:
            small_step(2 + k)
    total = acc[...]
    for k in range(3):
        z_c[k].wait_recv()
        total = total + zgot[k].astype(f32)
    out_ref[...] = total * factor
    for copy in sends:
        copy.wait_send()


def whole_call(frames, side, factor, sess, x, cot, read, w, sk, tk):
    _, rows, channels = x.shape
    depth = w.shape[0]
    taps = tk.shape[0]
    y_count = 3 + rows // (frames * side * side)
    vmem = pl.BlockSpec(memory_space=pltpu.VMEM)
    dma = pltpu.SemaphoreType.DMA
    bf16, f32 = jnp.bfloat16, jnp.float32
    wide = (depth, channels)
    return pl.pallas_call(
        functools.partial(whole_kernel, frames, side, factor),
        out_shape=[
            jax.ShapeDtypeStruct(wide, f32),
            jax.ShapeDtypeStruct(sk.shape, f32),
            jax.ShapeDtypeStruct(tk.shape, f32),
        ],
        in_specs=[pl.BlockSpec(memory_space=pltpu.SMEM)] + [vmem] * 6,
        out_specs=[vmem] * 3,
        scratch_shapes=[
            pltpu.VMEM(x.shape, bf16),
            pltpu.VMEM((2, 16) + wide, bf16),
            pltpu.VMEM((2,) + sk.shape, f32),
            pltpu.VMEM((2,) + tk.shape, f32),
            pltpu.VMEM((2, 4, 2, 2) + wide, bf16),
            pltpu.VMEM((2, 16, channels), f32),
            pltpu.VMEM((rows, channels), bf16),
            pltpu.VMEM((rows, channels), bf16),
            pltpu.VMEM((rows, channels), f32),
            pltpu.VMEM((rows, channels), bf16),
            pltpu.VMEM((9 + taps, frames, channels), f32),
            pltpu.VMEM((2, 4, 2) + wide, bf16),
            pltpu.VMEM((2, 4) + wide, bf16),
            pltpu.VMEM((2, 4) + wide, bf16),
            pltpu.VMEM(wide, f32),
            pltpu.VMEM((4,) + wide, bf16),
            pltpu.VMEM((4,) + wide, bf16),
            pltpu.VMEM((3,) + wide, bf16),
            pltpu.VMEM((3,) + wide, bf16),
            pltpu.VMEM((4, 16, channels), f32),
            pltpu.VMEM((5, 16, channels), f32),
        ]
        + [dma((n,)) for n in (y_count, y_count, 6, 6, 8, 8, 16, 16, 4)]
        + [dma((n,)) for n in (8, 8, 8, 8, 4, 4, 3, 3, 5, 5)],
        compiler_params=pltpu.CompilerParams(
            collective_id=0, has_side_effects=True, vmem_limit_bytes=48 << 20
        ),
        name="whole_backward",
    )(sess, x, cot, read, w, sk, tk)


def local(
    section_inputs, cotangent, sessions, point_weight, spatial_kernel, temporal_kernel, readout
):
    _, clip_count, frames, side, _, channels = section_inputs.shape
    cells = side * side

    def by_cell(block):
        last = block.shape[-1]
        return block.reshape(-1, frames, cells, last).transpose(0, 2, 1, 3).reshape(-1, last)

    halves = by_cell(section_inputs[0]).reshape(2, -1, channels)
    cot = by_cell(cotangent).reshape(2, -1, cotangent.shape[-1])
    factor = 1.0 / math.sqrt(clip_count * lax.axis_size("dp") * frames * cells)
    grads, s_out, t_out = whole_call(
        frames,
        side,
        factor,
        sessions,
        halves,
        cot,
        readout,
        point_weight[0],
        spatial_kernel.transpose(1, 0, 2),
        temporal_kernel.transpose(1, 0, 2),
    )
    return (grads[None], s_out.transpose(1, 0, 2), t_out.transpose(1, 0, 2))


def solution(mesh):
    halves = mesh.shape["section"] == 2 and mesh.shape["dp"] == 16
    return jax.shard_map(
        local if halves else pipelined,
        mesh=mesh,
        in_specs=(
            P("section", "dp", None, None, None, None),
            P("dp", None, None, None, None),
            P("dp"),
            P("section", "dp", None),
            P("section", None, None),
            P("section", None, None),
            P(),
        ),
        out_specs=(P("section", "dp", None), P("section", None, None), P("section", None, None)),
        check_vma=False,
    )
```

```python
import functools
import math

import jax
import jax.numpy as jnp
from jax import lax
from jax.experimental import pallas as pl
from jax.experimental.pallas import tpu as pltpu
from jax.sharding import PartitionSpec as P

INV_ROOT_TWO = 0.7071067811865476
INV_ROOT_TAU = 0.3989422804014327
LANES = 128
MESH = pl.DeviceIdType.MESH


def from_behind(block, axis, distance):
    devices = range(lax.axis_size(axis))
    route = [(i - distance, i) for i in devices if i - distance in devices]
    return lax.ppermute(block, axis, route)


def gelu_value(pre_act):
    return 0.5 * pre_act * (1.0 + jax.scipy.special.erf(pre_act * INV_ROOT_TWO))


def gelu_slope(pre_act):
    return (
        0.5 * (1.0 + jax.scipy.special.erf(pre_act * INV_ROOT_TWO))
        + pre_act * jnp.exp(-0.5 * pre_act * pre_act) * INV_ROOT_TAU
    )


def spatial_pad(field_in):
    pad_spec = [(0, 0)] * (field_in.ndim - 3) + [(1, 1), (1, 1), (0, 0)]
    return jnp.pad(field_in, pad_spec)


def spatial(field_in, kernel):
    height, width = (field_in.shape[-3], field_in.shape[-2])
    padded = spatial_pad(field_in)
    summed = jnp.zeros_like(field_in)
    for row_off in range(3):
        for col_off in range(3):
            summed = (
                summed
                + kernel[3 * row_off + col_off]
                * padded[..., row_off : row_off + height, col_off : col_off + width, :]
            )
    return summed


def spatial_back(grad_in, kernel):
    height, width = (grad_in.shape[-3], grad_in.shape[-2])
    padded = spatial_pad(grad_in)
    summed = jnp.zeros_like(grad_in)
    for row_off in range(3):
        for col_off in range(3):
            summed = (
                summed
                + kernel[3 * row_off + col_off]
                * padded[
                    ..., 2 - row_off : 2 - row_off + height, 2 - col_off : 2 - col_off + width, :
                ]
            )
    return summed


def spatial_kernel_grad(field_in, grad_in):
    height, width = (field_in.shape[-3], field_in.shape[-2])
    padded = spatial_pad(field_in)
    axes_all = tuple(range(field_in.ndim - 1))
    parts = []
    for row_off in range(3):
        for col_off in range(3):
            parts.append(
                jnp.sum(
                    padded[..., row_off : row_off + height, col_off : col_off + width, :] * grad_in,
                    axis=axes_all,
                )
            )
    return jnp.stack(parts)


def front_pad(field_in, tap_count):
    pad_spec = [(0, 0)] * (field_in.ndim - 4) + [(tap_count - 1, 0), (0, 0), (0, 0), (0, 0)]
    return jnp.pad(field_in, pad_spec)


def temporal(field_in, kernel):
    tap_count = kernel.shape[0]
    frames = field_in.shape[-4]
    padded = front_pad(field_in, tap_count)
    summed = jnp.zeros_like(field_in)
    for delay in range(tap_count):
        first = tap_count - 1 - delay
        summed = summed + kernel[delay] * padded[..., first : first + frames, :, :, :]
    return summed


def temporal_back(grad_in, kernel):
    tap_count = kernel.shape[0]
    frames = grad_in.shape[-4]
    pad_spec = [(0, 0)] * (grad_in.ndim - 4) + [(0, tap_count - 1), (0, 0), (0, 0), (0, 0)]
    padded = jnp.pad(grad_in, pad_spec)
    summed = jnp.zeros_like(grad_in)
    for delay in range(tap_count):
        summed = summed + kernel[delay] * padded[..., delay : delay + frames, :, :, :]
    return summed


def temporal_kernel_grad(field_in, grad_in, tap_count):
    frames = field_in.shape[-4]
    padded = front_pad(field_in, tap_count)
    axes_all = tuple(range(field_in.ndim - 1))
    parts = []
    for delay in range(tap_count):
        first = tap_count - 1 - delay
        parts.append(jnp.sum(padded[..., first : first + frames, :, :, :] * grad_in, axis=axes_all))
    return jnp.stack(parts)


def section_back(inputs, grad_out, s_kernel, t_kernel, hidden_of):
    field_in = inputs.astype(jnp.float32)
    spread = spatial(field_in, s_kernel)
    pre_act = temporal(spread, t_kernel)
    hidden = gelu_value(pre_act).astype(jnp.bfloat16)
    channels = inputs.shape[-1]
    flat_grad = grad_out.reshape(-1, channels)
    flat_hidden = hidden.reshape(-1, channels)
    hidden_grad = hidden_of(flat_grad).reshape(pre_act.shape)
    pre_grad = hidden_grad * gelu_slope(pre_act)
    spread_grad = temporal_back(pre_grad, t_kernel)
    in_grad = (grad_out.astype(jnp.float32) + spatial_back(spread_grad, s_kernel)).astype(
        jnp.bfloat16
    )
    weight_grad = jnp.dot(flat_hidden.T, flat_grad, preferred_element_type=jnp.float32)
    s_part = spatial_kernel_grad(field_in, spread_grad)
    t_part = temporal_kernel_grad(spread, pre_grad, t_kernel.shape[0])
    return (in_grad, weight_grad, s_part, t_part)


def pipelined(
    section_inputs, cotangent, sessions, point_weight, spatial_kernel, temporal_kernel, readout
):
    section_count = lax.axis_size("section")
    my_section = lax.axis_index("section")
    inputs = section_inputs[0]
    s_kernel = spatial_kernel[0]
    t_kernel = temporal_kernel[0]
    weight_shard = point_weight[0]
    clip_count = inputs.shape[0]
    channels = inputs.shape[-1]
    chosen = jnp.take(readout, sessions, axis=0)
    top_grads = jnp.einsum(
        "cfhwr,crk->cfhwk", cotangent, chosen, preferred_element_type=jnp.float32
    ).astype(jnp.bfloat16)
    block_size = 2
    step_count = clip_count // block_size
    tick_count = step_count + section_count - 1
    full_weight = lax.all_gather(weight_shard, "dp", axis=0, tiled=True)

    def hidden_of(flat_grad):
        return jnp.dot(flat_grad, full_weight.T, preferred_element_type=jnp.float32)

    block_shape = (block_size,) + inputs.shape[1:]

    def tick(tick_index, state_now):
        incoming, w_sum, s_sum, t_sum = state_now
        clip_step = tick_index - (section_count - 1 - my_section)
        is_live = (clip_step >= 0) & (clip_step < step_count)
        first_clip = jnp.clip(clip_step, 0, step_count - 1) * block_size
        inputs_block = lax.dynamic_slice_in_dim(inputs, first_clip, block_size, 0)
        top_block = lax.dynamic_slice_in_dim(top_grads, first_clip, block_size, 0)
        grad_out = jnp.where(my_section == section_count - 1, top_block, incoming)

        def live_work(sums):
            in_grad, w_part, s_part, t_part = section_back(
                inputs_block, grad_out, s_kernel, t_kernel, hidden_of
            )
            return (in_grad, sums[0] + w_part, sums[1] + s_part, sums[2] + t_part)

        def dead_work(sums):
            return (jnp.zeros(block_shape, jnp.bfloat16), sums[0], sums[1], sums[2])

        in_grad, w_new, s_new, t_new = lax.cond(
            is_live, live_work, dead_work, (w_sum, s_sum, t_sum)
        )
        passed = from_behind(in_grad, "section", -1)
        return (passed, w_new, s_new, t_new)

    start_state = (
        jnp.zeros(block_shape, jnp.bfloat16),
        jnp.zeros((channels, channels), jnp.float32),
        jnp.zeros((9, channels), jnp.float32),
        jnp.zeros(t_kernel.shape, jnp.float32),
    )
    finals = lax.fori_loop(0, tick_count, tick, start_state)
    weight_grads = lax.psum_scatter(finals[1], "dp", scatter_dimension=0, tiled=True)
    s_total, t_total = lax.psum((finals[2], finals[3]), "dp")
    rows_all = (
        clip_count * lax.axis_size("dp") * inputs.shape[1] * inputs.shape[2] * inputs.shape[3]
    )
    factor = 1.0 / math.sqrt(rows_all)
    return ((weight_grads * factor)[None], (s_total * factor)[None], (t_total * factor)[None])


def section_work(
    first, frames, side, x_ref, w_ref, sk_ref, tk_ref, wg_ref,
    st_ref, ing_ref, g_ref, hg_ref, hid_ref, acc_ref, middle, arrive
):
    taps = tk_ref.shape[0]
    cells = side * side
    clip_rows = cells * frames
    channels = x_ref.shape[1]
    rows = x_ref.shape[0]
    clips = rows // clip_rows
    hg_ref[...] = lax.dot_general(
        g_ref[...], w_ref[...].reshape(channels, channels), (((1,), (1,)), ((), ())), preferred_element_type=jnp.float32
    )
    acc_ref[...] = jnp.zeros_like(acc_ref)
    frame_of = lax.broadcasted_iota(jnp.int32, (frames, LANES), 0)
    chunks = channels // LANES

    def step(index, carry):
        clip = index // chunks
        lanes = pl.ds(pl.multiple_of((index % chunks) * LANES, LANES), LANES)
        span = pl.ds(pl.multiple_of(clip * clip_rows, clip_rows), clip_rows)

        def tile(value):
            return jnp.broadcast_to(value, (frames, LANES))

        s_taps = [tile(sk_ref[k, :, lanes]) for k in range(9)]
        t_taps = [tile(tk_ref[d, :, lanes]) for d in range(taps)]
        t_front = [jnp.where(frame_of >= d, t_taps[d], 0.0) for d in range(taps)]
        t_tail = [jnp.where(frame_of < frames - d, t_taps[d], 0.0) for d in range(taps)]
        x_all = x_ref[span, lanes].astype(jnp.float32)
        hg_all = hg_ref[span, lanes]
        x = [x_all[c * frames : (c + 1) * frames] for c in range(cells)]
        inside = lambda i, j: 0 <= i < side and 0 <= j < side
        spread, sgrad, hidden = [], [], []
        t_sums = [None] * taps
        for i in range(side):
            for j in range(side):
                total = None
                for r in range(3):
                    for q in range(3):
                        if inside(i + r - 1, j + q - 1):
                            term = s_taps[3 * r + q] * x[(i + r - 1) * side + j + q - 1]
                            total = term if total is None else total + term
                pre = t_taps[0] * total
                for d in range(1, taps):
                    pre = pre + t_front[d] * pltpu.roll(total, d, 0)
                half = 0.5 + 0.5 * lax.erf(pre * INV_ROOT_TWO)
                hidden.append(pre * half)
                slope = half + pre * jnp.exp(-0.5 * pre * pre) * INV_ROOT_TAU
                c = i * side + j
                pgrad = hg_all[c * frames : (c + 1) * frames] * slope
                back = t_taps[0] * pgrad
                for d in range(taps):
                    moved = pgrad if d == 0 else pltpu.roll(pgrad, frames - d, 0)
                    if d:
                        back = back + t_tail[d] * moved
                    part = total * moved
                    t_sums[d] = part if t_sums[d] is None else t_sums[d] + part
                sgrad.append(back)
        hid_ref[span, lanes] = jnp.concatenate(hidden, axis=0).astype(jnp.bfloat16)
        for d in range(taps):
            acc_ref[9 + d, :, lanes] += t_sums[d]
        s_sums = [None] * 9
        for i in range(side):
            for j in range(side):
                for r in range(3):
                    for q in range(3):
                        if inside(i + r - 1, j + q - 1):
                            part = x[(i + r - 1) * side + j + q - 1] * sgrad[i * side + j]
                            k = 3 * r + q
                            s_sums[k] = part if s_sums[k] is None else s_sums[k] + part
        for k in range(9):
            acc_ref[k, :, lanes] += s_sums[k]
        if first:
            out = []
            for i in range(side):
                for j in range(side):
                    total = None
                    for r in range(3):
                        for q in range(3):
                            if inside(i - r + 1, j - q + 1):
                                term = s_taps[3 * r + q] * sgrad[(i - r + 1) * side + j - q + 1]
                                total = term if total is None else total + term
                    out.append(total)
            ing_ref[span, lanes] = (
                g_ref[span, lanes].astype(jnp.float32) + jnp.concatenate(out, axis=0)
            ).astype(jnp.bfloat16)
        return carry


    def clip_step(clip, carry):
        arrive(clip)
        return lax.fori_loop(
            0, chunks, lambda index, kept: step(clip * chunks + index, kept), carry
        )

    lax.fori_loop(0, clips // 2, clip_step, 0)
    middle()
    lax.fori_loop(clips // 2, clips, clip_step, 0)
    wg = lax.dot_general(
        hid_ref[...], g_ref[...], (((0,), (0,)), ((), ())), preferred_element_type=jnp.float32
    )
    wg_ref[...] = wg.astype(wg_ref.dtype).reshape(wg_ref.shape)
    wide = lax.broadcasted_iota(jnp.int32, (frames, channels), 0)
    st_ref[...] = jnp.zeros_like(st_ref)
    for k in range(9):
        st_ref[k : k + 1, :] = jnp.sum(acc_ref[k], axis=0, keepdims=True)
    for d in range(taps):
        kept = jnp.where(wide < frames - d, acc_ref[9 + d], 0.0)
        st_ref[9 + d : 10 + d, :] = jnp.sum(kept, axis=0, keepdims=True)


def places():
    dp = lax.axis_index("dp")
    sec = lax.axis_index("section")
    return dp, sec, dp // 4, (dp // 2) % 2, dp % 2


def greet(partners):
    barrier = pltpu.get_barrier_semaphore()
    for there in partners:
        pl.semaphore_signal(barrier, inc=1, device_id=there, device_id_type=MESH)
    pl.semaphore_wait(barrier, len(partners))


def remote(src, dst, sems, slot, there):
    return pltpu.make_async_remote_copy(
        src_ref=src,
        dst_ref=dst,
        send_sem=sems[0].at[slot],
        recv_sem=sems[1].at[slot],
        device_id=there,
        device_id_type=MESH,
    )


def whole_kernel(
    frames,
    side,
    factor,
    sess_ref,
    x_ref,
    cot_ref,
    read_ref,
    w_ref,
    sk_ref,
    tk_ref,
    out_ref,
    so_ref,
    to_ref,
    *scratch,
):
    xo_ref, wo_ref, sko_ref, tko_ref, wg_ref, st_ref = scratch[:6]
    work = scratch[6:11]
    cgot, xsend, xgot, acc, ysend, ygot, zsend, zgot, ssend, sgot = scratch[11:21]
    ays, ayr, azs, azr, axs, axr, acs, acr, own_sem = scratch[21:30]
    cs, cr, xs, xr, ys, yr, zs, zr, ss, sr = scratch[30:]
    f32, bf16 = jnp.float32, jnp.bfloat16
    taps = tk_ref.shape[0]
    channels = w_ref.shape[1]
    dp, sec, z, x, c = places()
    over = (dp, 1 - sec)
    mate = (z * 4 + x * 2 + 1 - c, sec)
    side_chip = (z * 4 + (1 - x) * 2 + c, sec)
    line = [((z + h) % 4 * 4 + x * 2 + c, sec) for h in (1, 2, 3)]
    greet([over, mate, side_chip] + line)
    secs = (sec, 1 - sec)
    block = [(z + 1 + k) % 4 for k in range(4)]
    sends = []

    def go(src, dst, sems, slot, there):
        copy = remote(src, dst, sems, slot, there)
        copy.start()
        sends.append(copy)
        return copy

    slot_of = wo_ref.at[sec, dp]
    y_w = go(w_ref, slot_of, (ays, ayr), 0, over)
    z_w = {}
    x_w = {}
    c_w = {}
    for h in range(3):
        z_w[0, h] = go(w_ref, slot_of, (azs, azr), h, line[h])
    x_w[0, 0] = go(w_ref, slot_of, (axs, axr), 0, side_chip)
    c_w[0, 0] = go(w_ref, slot_of, (acs, acr), 0, mate)
    y_rest = [
        go(sk_ref, sko_ref.at[sec], (ays, ayr), 1, over),
        go(tk_ref, tko_ref.at[sec], (ays, ayr), 2, over),
    ]
    clip_rows = side * side * frames
    clips = x_ref.shape[1] // clip_rows

    def clip_copy(clip):
        span = pl.ds(pl.multiple_of(clip * clip_rows, clip_rows), clip_rows)
        return remote(
            x_ref.at[1 - sec, span], xo_ref.at[sec, span], (ays, ayr), 3 + clip, over
        )

    for clip in range(clips):
        copy = clip_copy(clip)
        copy.start()
        sends.append(copy)
    kept = [
        pltpu.make_async_copy(w_ref, slot_of, own_sem.at[0]),
        pltpu.make_async_copy(sk_ref, sko_ref.at[sec], own_sem.at[1]),
        pltpu.make_async_copy(tk_ref, tko_ref.at[sec], own_sem.at[2]),
        pltpu.make_async_copy(x_ref.at[sec], xo_ref.at[sec], own_sem.at[3]),
    ]
    for copy in kept:
        copy.start()
    y_w.wait_recv()
    held = wo_ref.at[1 - sec, dp]
    for h in range(3):
        z_w[1, h] = go(held, held, (azs, azr), 3 + h, line[h])
    x_w[1, 0] = go(held, held, (axs, axr), 4, side_chip)
    c_w[1, 0] = go(held, held, (acs, acr), 8, mate)

    def slot_copy(s, source, sems, base, h, there):
        kind = (s + sec) % 2
        held = wo_ref.at[s, source]
        return remote(held, held, sems, base * kind + h, there)

    def pass_on(copy):
        copy.start()
        sends.append(copy)

    def from_line(s, h):
        source = (z + 3 - h) % 4 * 4 + x * 2 + c
        slot_copy(s, source, (azs, azr), 3, h, line[h]).wait_recv()
        pass_on(slot_copy(s, source, (axs, axr), 4, h + 1, side_chip))
        pass_on(slot_copy(s, source, (acs, acr), 8, h + 1, mate))

    def from_side(s):
        for h in range(4):
            source = (z + 4 - h) % 4 * 4 + (1 - x) * 2 + c
            slot_copy(s, source, (axs, axr), 4, h, side_chip).wait_recv()
            pass_on(slot_copy(s, source, (acs, acr), 8, h + 4, mate))

    def from_mate(s):
        for h in range(8):
            slot_copy(s, dp, (acs, acr), 8, h, mate).wait_recv()

    top_ref = work[1]
    for clip in range(clips):
        span = pl.ds(clip * clip_rows, clip_rows)
        top_ref[span, :] = jnp.dot(
            cot_ref[sec, span, :],
            read_ref[sess_ref[sec * clips + clip]],
            preferred_element_type=jnp.float32,
        ).astype(bf16)
    for h in range(3):
        from_line(1, h)
        from_line(0, h)
    from_side(1)
    from_mate(1)
    for copy in y_rest:
        copy.wait_recv()
    for copy in kept:
        copy.wait()

    def compute(s, middle):
        def arrive(clip):
            @pl.when(sec != s)
            def _():
                clip_copy(clip).wait_recv()

        ing_ref, g_ref, hg_ref, hid_ref, acc_ref = work
        section_work(
            s == 1,
            frames,
            side,
            xo_ref.at[s],
            wo_ref.at[s],
            sko_ref.at[s],
            tko_ref.at[s],
            wg_ref.at[s],
            st_ref.at[s],
            ing_ref,
            g_ref if s == 1 else ing_ref,
            hg_ref,
            hid_ref,
            acc_ref,
            middle,
            arrive,
        )

    core = {}

    def core_stage(s):
        for k in range(4):
            core[s, k] = go(
                wg_ref.at[s, block[k], :, 1 - c], cgot.at[s, k], (cs, cr), 4 * s + k, mate
            )

    def x_stage(s):
        for k in range(4):
            core[s, k].wait_recv()
            xsend[s, k] = (
                wg_ref[s, block[k], 1 - x, c].astype(f32) + cgot[s, k, 1 - x].astype(f32)
            ).astype(bf16)
            go(xsend.at[s, k], xgot.at[s, k], (xs, xr), 4 * s + k, side_chip)

    compute(1, lambda: from_side(0))
    core_stage(1)
    from_mate(0)
    compute(0, lambda: x_stage(1))
    core_stage(0)
    small = [go(st_ref.at[1 - sec], sgot.at[0], (ss, sr), 0, over)]
    small_to = [mate, side_chip, (dp + 4 - 8 * (z % 2), sec), ((dp + 8) % 16, sec)]

    def small_step(n):
        small[n].wait_recv()
        value = (st_ref[sec] if n == 0 else ssend[n - 1]) + sgot[n]
        if n == 4:
            value = value * factor
            for k in range(9):
                so_ref[k] = value[k : k + 1]
            for d in range(taps):
                to_ref[d] = value[9 + d : 10 + d]
        else:
            ssend[n] = value
            small.append(go(ssend.at[n], sgot.at[n + 1], (ss, sr), n + 1, small_to[n]))

    x_stage(0)

    def chip_pair_sum(s, k):
        remote(xsend.at[s, k], xgot.at[s, k], (xs, xr), 4 * s + k, side_chip).wait_recv()
        return (
            wg_ref[s, block[k], x, c].astype(f32)
            + cgot[s, k, x].astype(f32)
            + xgot[s, k].astype(f32)
        )

    y_c = []
    for k in range(4):
        ysend[k] = chip_pair_sum(1 - sec, k).astype(bf16)
        y_c.append(go(ysend.at[k], ygot.at[k], (ys, yr), k, over))
        if k % 2:
            small_step(k // 2)
    z_c = []
    for k in range(4):
        value = chip_pair_sum(sec, k)
        y_c[k].wait_recv()
        value = value + ygot[k].astype(f32)
        if k < 3:
            zsend[k] = value.astype(bf16)
            z_c.append(go(zsend.at[k], zgot.at[k], (zs, zr), k, line[k]))
        else:
            acc[...] = value
        if k < 3:
            small_step(2 + k)
    total = acc[...]
    for k in range(3):
        z_c[k].wait_recv()
        total = total + zgot[k].astype(f32)
    out_ref[...] = total * factor
    for copy in sends:
        copy.wait_send()


def whole_call(frames, side, factor, sess, x, cot, read, w, sk, tk):
    _, rows, channels = x.shape
    depth = w.shape[0]
    taps = tk.shape[0]
    y_count = 3 + rows // (frames * side * side)
    vmem = pl.BlockSpec(memory_space=pltpu.VMEM)
    dma = pltpu.SemaphoreType.DMA
    bf16, f32 = jnp.bfloat16, jnp.float32
    wide = (depth, channels)
    return pl.pallas_call(
        functools.partial(whole_kernel, frames, side, factor),
        out_shape=[
            jax.ShapeDtypeStruct(wide, f32),
            jax.ShapeDtypeStruct(sk.shape, f32),
            jax.ShapeDtypeStruct(tk.shape, f32),
        ],
        in_specs=[pl.BlockSpec(memory_space=pltpu.SMEM)] + [vmem] * 6,
        out_specs=[vmem] * 3,
        scratch_shapes=[
            pltpu.VMEM(x.shape, bf16),
            pltpu.VMEM((2, 16) + wide, bf16),
            pltpu.VMEM((2,) + sk.shape, f32),
            pltpu.VMEM((2,) + tk.shape, f32),
            pltpu.VMEM((2, 4, 2, 2) + wide, bf16),
            pltpu.VMEM((2, 16, channels), f32),
            pltpu.VMEM((rows, channels), bf16),
            pltpu.VMEM((rows, channels), bf16),
            pltpu.VMEM((rows, channels), f32),
            pltpu.VMEM((rows, channels), bf16),
            pltpu.VMEM((9 + taps, frames, channels), f32),
            pltpu.VMEM((2, 4, 2) + wide, bf16),
            pltpu.VMEM((2, 4) + wide, bf16),
            pltpu.VMEM((2, 4) + wide, bf16),
            pltpu.VMEM(wide, f32),
            pltpu.VMEM((4,) + wide, bf16),
            pltpu.VMEM((4,) + wide, bf16),
            pltpu.VMEM((3,) + wide, bf16),
            pltpu.VMEM((3,) + wide, bf16),
            pltpu.VMEM((4, 16, channels), f32),
            pltpu.VMEM((5, 16, channels), f32),
        ]
        + [dma((n,)) for n in (y_count, y_count, 6, 6, 8, 8, 16, 16, 4)]
        + [dma((n,)) for n in (8, 8, 8, 8, 4, 4, 3, 3, 5, 5)],
        compiler_params=pltpu.CompilerParams(
            collective_id=0, has_side_effects=True, vmem_limit_bytes=48 << 20
        ),
        name="whole_backward",
    )(sess, x, cot, read, w, sk, tk)


def local(
    section_inputs, cotangent, sessions, point_weight, spatial_kernel, temporal_kernel, readout
):
    _, clip_count, frames, side, _, channels = section_inputs.shape
    cells = side * side

    def by_cell(block):
        last = block.shape[-1]
        return block.reshape(-1, frames, cells, last).transpose(0, 2, 1, 3).reshape(-1, last)

    halves = by_cell(section_inputs[0]).reshape(2, -1, channels)
    cot = by_cell(cotangent).reshape(2, -1, cotangent.shape[-1])
    factor = 1.0 / math.sqrt(clip_count * lax.axis_size("dp") * frames * cells)
    grads, s_out, t_out = whole_call(
        frames,
        side,
        factor,
        sessions,
        halves,
        cot,
        readout,
        point_weight[0],
        spatial_kernel.transpose(1, 0, 2),
        temporal_kernel.transpose(1, 0, 2),
    )
    return (grads[None], s_out.transpose(1, 0, 2), t_out.transpose(1, 0, 2))


def solution(mesh):
    halves = mesh.shape["section"] == 2 and mesh.shape["dp"] == 16
    return jax.shard_map(
        local if halves else pipelined,
        mesh=mesh,
        in_specs=(
            P("section", "dp", None, None, None, None),
            P("dp", None, None, None, None),
            P("dp"),
            P("section", "dp", None),
            P("section", None, None),
            P("section", None, None),
            P(),
        ),
        out_specs=(P("section", "dp", None), P("section", None, None), P("section", None, None)),
        check_vma=False,
    )
```
